32 devices in a mesh: groups: 2 (over y), sample: 4 (over z), fsdp: 2 (over x), prompt: 2 (over core).
Axes of the slice: x: 2, y: 2, z: 4, core: 2. Of those that a mesh axis runs over, the one named last changes fastest.
Arguments:
- queries: bfloat16 [4, 4, 256, 4096], P(('groups', 'prompt'), 'sample', 'fsdp'), parts along dimension 0, may hold values from -16 to 16
- completion_keys: bfloat16 [4, 4, 256, 512], P(('groups', 'prompt'), 'sample', 'fsdp'), parts along dimension 0, may hold values from -6 to 6
- completion_values: bfloat16 [4, 4, 256, 512], P(('groups', 'prompt'), 'sample', 'fsdp'), parts along dimension 0, may hold values from -6 to 6
- prompt_keys: bfloat16 [4, 8, 512], P(('groups', 'prompt'), ('sample', 'fsdp')), parts along dimension 0, may hold values from -6 to 6
- prompt_values: bfloat16 [4, 8, 512], P(('groups', 'prompt'), ('sample', 'fsdp')), parts along dimension 0, may hold values from -6 to 6
- output_grad: bfloat16 [4, 4, 256, 4096], P(('groups', 'prompt'), 'sample', 'fsdp'), parts along dimension 0, may hold values from -6 to 6
- lengths: int32 [4, 4], P(('groups', 'prompt'), 'sample'), parts along dimension 0, may hold values from 64 to 256
Outputs:
- attention_out: bfloat16 [4, 4, 256, 4096], P(('groups', 'prompt'), 'sample', 'fsdp'), parts along dimension 0
- query_grad: bfloat16 [4, 4, 256, 4096], P(('groups', 'prompt'), 'sample', 'fsdp'), parts along dimension 0
- completion_key_grad: float32 [4, 4, 256, 512], P(('groups', 'prompt'), 'sample', 'fsdp'), parts along dimension 0
- completion_value_grad: float32 [4, 4, 256, 512], P(('groups', 'prompt'), 'sample', 'fsdp'), parts along dimension 0
- shared_prompt_key_gradient: float32 [4, 8, 512], P(('groups', 'prompt'), ('sample', 'fsdp')), parts along dimension 0
- shared_prompt_value_gradient: float32 [4, 8, 512], P(('groups', 'prompt'), ('sample', 'fsdp')), parts along dimension 0
The draws below stay inside these ranges and needn't reach their ends.
There are 2 independent parts, one for each index of `groups`. The reference program is written for one: setup_inputs(seed, part) draws one part's arguments, and reference() takes and returns one part's arrays. A program takes and returns all parts, laid end to end along the dimension named above; each array names one. Nothing has to cross between parts.
All inputs are finite; a program needn't handle non-finite values.
Results may differ from the reference program's by a relative error of at most 0.02.
Values may be sent and summed in bfloat16 or wider, within the bound.
No kernel may reach another device: no remote copies, remote signals or barrier semaphores. Data moves between devices by JAX's collectives and lax.ppermute only.
A program may use at most 128 MiB of HBM per device.

```python
import jax
import jax.numpy as jnp
from jax import lax

HEADS = 32
KV_HEADS = 4
HEAD_DIM = 128
COMP_LEN = 256
PROMPT_LEN = 8
COMPLETIONS = 4


def draw_prompt_keys(key, part):
    noise_key = jax.random.fold_in(key, 31)
    drawn = jnp.clip(jax.random.normal(noise_key, (2, PROMPT_LEN, KV_HEADS * HEAD_DIM), jnp.float32), -6.0, 6.0)
    return drawn.astype(jnp.bfloat16)


def draw_queries(key, part):
    noise_key = jax.random.fold_in(key, 47)
    shape = (2, COMPLETIONS, COMP_LEN, HEADS * HEAD_DIM)
    drawn = jnp.clip(jax.random.normal(noise_key, shape, jnp.float32), -6.0, 6.0)
    return drawn.astype(jnp.bfloat16)


def with_ends(values, stream_key, least, largest):
    dims = values.shape
    index_at = [jax.random.randint(jax.random.fold_in(stream_key, axis), (), 0, dims[axis]) for axis in range(len(dims))]
    values = values.at[tuple(index_at)].set(least)
    longest = dims.index(max(dims))
    index_at[longest] = (index_at[longest] + 1) % dims[longest]
    return values.at[tuple(index_at)].set(largest)


def steps_of(key, dims, shards, least, high):
    factor_of = 1.0
    for dim, shards_of in shards:
        heights = jax.random.uniform(jax.random.fold_in(jax.random.fold_in(key, 6), dim), (shards_of,), jnp.float32, least / len(shards), high / len(shards))
        factor_of = factor_of * jnp.repeat(jnp.exp(heights), dims[dim] // shards_of).reshape((-1,) + (1,) * (len(dims) - 1 - dim))
    return factor_of


def scatter_about(stream_key, extent, width, limit, cuts=(), kind=jnp.bfloat16):
    array = jax.random.normal(stream_key, extent, jnp.float32) * width
    if len(cuts) > 0:
        array = steps_of(stream_key, extent, cuts, -0.22, 0.18) * array
    return jnp.clip(array, min=-limit, max=limit).astype(kind)


def setup_inputs(seed: int = 0, part: int = 0) -> dict:
    arg_keys = jax.random.split(jax.random.key(seed), 8)
    part_splits = jax.random.split(jax.random.fold_in(arg_keys[7], part), 8)
    return {
        "queries": draw_queries(jax.random.fold_in(jax.random.fold_in(arg_keys[7], part), 71), part),
        "completion_keys": scatter_about(part_splits[1], (2, COMPLETIONS, COMP_LEN, KV_HEADS * HEAD_DIM), 1.0, 6.0, ((0, 2), (1, 4), (2, 2))),
        "completion_values": scatter_about(part_splits[2], (2, COMPLETIONS, COMP_LEN, KV_HEADS * HEAD_DIM), 1.0, 6.0, ((0, 2), (1, 4), (2, 2))),
        "prompt_keys": draw_prompt_keys(jax.random.fold_in(jax.random.fold_in(arg_keys[7], part), 71), part),
        "prompt_values": scatter_about(part_splits[4], (2, PROMPT_LEN, KV_HEADS * HEAD_DIM), 1.0, 6.0, ((0, 2), (1, 8))),
        "output_grad": scatter_about(part_splits[5], (2, COMPLETIONS, COMP_LEN, HEADS * HEAD_DIM), 1.0, 6.0, ((0, 2), (1, 4), (2, 2))),
        "lengths": with_ends(jax.random.randint(part_splits[6], (2, COMPLETIONS), COMP_LEN // 4, COMP_LEN + 1), jax.random.fold_in(part_splits[6], 1), COMP_LEN // 4, COMP_LEN).astype(jnp.int32),
    }


def attend(query_rows, grad_input, length, prompt_keys, prompt_values, own_keys, own_values):
    prompt_span = prompt_keys.shape[0]
    comp_span = query_rows.shape[0]
    group_share = HEADS // KV_HEADS
    softmax_scale = HEAD_DIM ** -0.5
    key_data = jnp.concatenate([prompt_keys, own_keys], 0).reshape(-1, KV_HEADS, HEAD_DIM).astype(jnp.float32)
    value_data = jnp.concatenate([prompt_values, own_values], 0).reshape(-1, KV_HEADS, HEAD_DIM).astype(jnp.float32)
    query_data = query_rows.reshape(comp_span, KV_HEADS, group_share, HEAD_DIM).astype(jnp.float32)
    token_pos = jnp.arange(comp_span, dtype=jnp.int32)
    key_pos = jnp.arange(prompt_span + comp_span, dtype=jnp.int32)
    visible = (key_pos[None, :] < prompt_span) | (key_pos[None, :] - prompt_span <= token_pos[:, None])
    scores = jnp.einsum("tgrd,jgd->grtj", query_data, key_data) * softmax_scale
    scores = jnp.where(visible[None, None], scores, -jnp.inf)
    maximum = jnp.max(scores, axis=-1, keepdims=True)
    exponent = jnp.exp(scores - maximum)
    attention = exponent / jnp.sum(exponent, axis=-1, keepdims=True)
    attention_half = lax.optimization_barrier(attention.astype(jnp.bfloat16)).astype(jnp.float32)
    blended_output = jnp.einsum("grtj,jgd->tgrd", attention_half, value_data).astype(jnp.bfloat16)
    token_weight = jnp.where(token_pos < length, jnp.float32(comp_span) / length.astype(jnp.float32), jnp.float32(0.0))
    gradient_row_slice = (grad_input.astype(jnp.float32) * token_weight[:, None]).astype(jnp.bfloat16)
    gradient_tensor = lax.optimization_barrier(gradient_row_slice).astype(jnp.float32).reshape(comp_span, KV_HEADS, group_share, HEAD_DIM)
    row_inner_product = jnp.einsum("keqf,keqf->eqk", gradient_tensor, blended_output.astype(jnp.float32))
    prob_grad = jnp.einsum("tgrd,jgd->grtj", gradient_tensor, value_data)
    score_grad = (attention * (prob_grad - row_inner_product[..., None])).astype(jnp.bfloat16)
    score_grad = lax.optimization_barrier(score_grad).astype(jnp.float32)
    query_grad = (jnp.einsum("grtj,jgd->tgrd", score_grad, key_data) * softmax_scale).astype(jnp.bfloat16)
    key_grad = jnp.einsum("grtj,tgrd->jgd", score_grad, query_data) * softmax_scale
    value_grad = jnp.einsum("grtj,tgrd->jgd", attention_half, gradient_tensor)
    total = prompt_span + comp_span
    return (blended_output.reshape(comp_span, HEADS * HEAD_DIM), query_grad.reshape(comp_span, HEADS * HEAD_DIM),
            key_grad.reshape(total, KV_HEADS * HEAD_DIM), value_grad.reshape(total, KV_HEADS * HEAD_DIM))


def reference(queries, completion_keys, completion_values, prompt_keys, prompt_values, output_grad, lengths):
    mixed_all, query_all, own_key_all, own_value_all, prompt_key_all, prompt_value_all = [], [], [], [], [], []
    for prompt_index in range(2):
        def per_completion(items):
            return attend(items[0], items[1], items[2], prompt_keys[prompt_index], prompt_values[prompt_index], items[3], items[4])

        results = lax.map(per_completion, (queries[prompt_index], output_grad[prompt_index], lengths[prompt_index],
                                           completion_keys[prompt_index], completion_values[prompt_index]))
        mixed_all.append(results[0])
        query_all.append(results[1])
        own_key_all.append(results[2][:, PROMPT_LEN:])
        own_value_all.append(results[3][:, PROMPT_LEN:])
        prompt_key_all.append(jnp.sum(results[2][:, :PROMPT_LEN], axis=0))
        prompt_value_all.append(jnp.sum(results[3][:, :PROMPT_LEN], axis=0))
    return (jnp.stack(mixed_all), jnp.stack(query_all), jnp.stack(own_key_all), jnp.stack(own_value_all),
            jnp.stack(prompt_key_all), jnp.stack(prompt_value_all))
```

```python
import functools

import jax
import jax.numpy as jnp
from jax import lax
from jax.experimental import pallas as pl
from jax.experimental.pallas import tpu as pltpu
from jax.sharding import PartitionSpec as P

HEAD_DIM = 128
LOG2E = 1.4426950408889634

NT = (((1,), (1,)), ((), ()))
NN = (((1,), (0,)), ((), ()))


def mm(a, b, dims=NN):
    return lax.dot_general(a, b, dims, preferred_element_type=jnp.float32)


def pad_rows(x, rows):
    if x.shape[0] == rows:
        return x
    return jnp.concatenate([x, jnp.zeros((rows - x.shape[0], x.shape[1]), x.dtype)], 0)


def attend_kernel(shifts, share, comp_span, scal, q_ref, g_ref, k_ref, v_ref, *refs):
    earlier = refs[: 2 * shifts]
    prefix, out, dq, dk, dv = refs[2 * shifts : 2 * shifts + 5]
    rest = refs[2 * shifts + 5 :]
    if shifts:
        dback, dprefix, probs_s, grads_s = rest
    else:
        dprefix, probs_s, grads_s = rest
    rows = q_ref.shape[0]
    prompt = prefix.shape[0]
    padded = -(-prompt // 16) * 16
    place, length = scal[0], scal[1]
    scale = HEAD_DIM ** -0.5
    factor = scale * LOG2E

    token = place * rows + lax.broadcasted_iota(jnp.int32, (rows, 1), 0)
    weight = jnp.where(
        token < length, jnp.float32(comp_span) / length.astype(jnp.float32), jnp.float32(0.0)
    )
    weight = jnp.broadcast_to(weight, (rows, HEAD_DIM))
    prefix_k = pad_rows(prefix[:, 0, :], padded).astype(jnp.bfloat16)
    prefix_v = pad_rows(prefix[:, 1, :], padded).astype(jnp.bfloat16)
    keys = jnp.concatenate([k_ref[...]] + [earlier[2 * s][...] for s in range(shifts)] + [prefix_k], 0)
    values = jnp.concatenate(
        [v_ref[...]] + [earlier[2 * s + 1][...] for s in range(shifts)] + [prefix_v], 0
    )
    comp = rows * (1 + shifts)
    keys_t = keys.astype(jnp.float32).T.astype(jnp.bfloat16)
    values_t = values.astype(jnp.float32).T.astype(jnp.bfloat16)
    key_row = lax.broadcasted_iota(jnp.int32, (rows, rows), 0)
    token_col = lax.broadcasted_iota(jnp.int32, (rows, rows), 1)
    causal = key_row <= token_col
    heads = 2 if share % 2 == 0 else 1
    causal = jnp.concatenate([causal] * heads, 1)
    neg = jnp.float32(-jnp.inf)
    pad_mask = lax.broadcasted_iota(jnp.int32, (padded, heads * rows), 0) < prompt
    bias = [jnp.where(place >= s + 1, jnp.float32(0.0), neg) for s in range(shifts)]

    for first in range(0, share, heads):
        span = [slice((first + h) * HEAD_DIM, (first + h + 1) * HEAD_DIM) for h in range(heads)]
        q = jnp.concatenate([q_ref[:, c] for c in span], 0)
        g = jnp.concatenate(
            [(g_ref[:, c].astype(jnp.float32) * weight).astype(jnp.bfloat16) for c in span], 0
        )
        scores = mm(keys, q, NT)
        dprob = mm(values, g, NT)
        own = jnp.where(causal, scores[:rows], neg)
        back = [scores[rows * (1 + s) : rows * (2 + s)] for s in range(shifts)]
        lead = scores[comp:]
        if padded != prompt:
            lead = jnp.where(pad_mask, lead, neg)
        top = jnp.maximum(jnp.max(own, 0, keepdims=True), jnp.max(lead, 0, keepdims=True))
        for s in range(shifts):
            top = jnp.maximum(top, jnp.max(back[s], 0, keepdims=True) + bias[s])
        top = top * factor
        parts = [jnp.exp2(own * factor - top)]
        parts += [jnp.exp2(back[s] * factor - (top - bias[s])) for s in range(shifts)]
        parts += [jnp.exp2(lead * factor - top)]
        expo = jnp.concatenate(parts, 0)
        inverse = 1.0 / jnp.sum(expo, 0, keepdims=True)
        dot = jnp.sum(expo * dprob, 0, keepdims=True) * inverse
        probs = expo * inverse
        sgrad = (probs * (dprob - dot)).astype(jnp.bfloat16)
        probs = probs.astype(jnp.bfloat16)
        cols = slice(first * rows, (first + heads) * rows)
        probs_s[:, cols] = probs
        grads_s[:, cols] = sgrad
        mixed = mm(values_t[:, :comp], probs[:comp]) + mm(values_t[:, comp:], probs[comp:])
        dquery = (mm(keys_t[:, :comp], sgrad[:comp]) + mm(keys_t[:, comp:], sgrad[comp:])) * scale
        for h, c in enumerate(span):
            t = slice(h * rows, (h + 1) * rows)
            out[:, c] = mixed[:, t].T.astype(jnp.bfloat16)
            dq[:, c] = dquery[:, t].T.astype(jnp.bfloat16)

    q = jnp.concatenate([q_ref[:, h * HEAD_DIM : (h + 1) * HEAD_DIM] for h in range(share)], 0)
    g = jnp.concatenate(
        [
            (g_ref[:, h * HEAD_DIM : (h + 1) * HEAD_DIM].astype(jnp.float32) * weight).astype(jnp.bfloat16)
            for h in range(share)
        ],
        0,
    )
    key_term = mm(grads_s[...], q) * scale
    value_term = mm(probs_s[...], g)
    dk[...] = key_term[:rows]
    dv[...] = value_term[:rows]
    for s in range(shifts):
        dback[s, 0] = key_term[rows * (1 + s) : rows * (2 + s)].astype(jnp.bfloat16)
        dback[s, 1] = value_term[rows * (1 + s) : rows * (2 + s)].astype(jnp.bfloat16)
    dprefix[:, 0, :] = key_term[comp : comp + prompt]
    dprefix[:, 1, :] = value_term[comp : comp + prompt]


def attend(scal, queries, grads, keys, values, earlier, prefix, comp_span):
    rows, width = queries.shape
    groups = keys.shape[1] // HEAD_DIM
    share = width // HEAD_DIM // groups
    shifts = len(earlier) // 2
    prompt = prefix.shape[0]
    padded = -(-prompt // 16) * 16
    total = rows * (1 + shifts) + padded
    wide = pl.BlockSpec((rows, share * HEAD_DIM), lambda i, s: (0, i))
    narrow = pl.BlockSpec((rows, HEAD_DIM), lambda i, s: (0, i))
    lead = pl.BlockSpec((prompt, 2, HEAD_DIM), lambda i, s: (0, 0, i))
    outs = [
        jax.ShapeDtypeStruct((rows, width), jnp.bfloat16),
        jax.ShapeDtypeStruct((rows, width), jnp.bfloat16),
        jax.ShapeDtypeStruct(keys.shape, jnp.float32),
        jax.ShapeDtypeStruct(keys.shape, jnp.float32),
    ]
    out_specs = [wide, wide, narrow, narrow]
    if shifts:
        outs.append(jax.ShapeDtypeStruct((shifts, 2) + keys.shape, jnp.bfloat16))
        out_specs.append(pl.BlockSpec((shifts, 2, rows, HEAD_DIM), lambda i, s: (0, 0, 0, i)))
    outs.append(jax.ShapeDtypeStruct(prefix.shape, jnp.float32))
    out_specs.append(lead)
    result = pl.pallas_call(
        functools.partial(attend_kernel, shifts, share, comp_span),
        out_shape=outs,
        grid_spec=pltpu.PrefetchScalarGridSpec(
            num_scalar_prefetch=1,
            grid=(groups,),
            in_specs=[wide, wide, narrow, narrow] + [narrow] * (2 * shifts) + [lead],
            out_specs=out_specs,
            scratch_shapes=[
                pltpu.VMEM((total, share * rows), jnp.bfloat16),
                pltpu.VMEM((total, share * rows), jnp.bfloat16),
            ],
        ),
        compiler_params=pltpu.CompilerParams(dimension_semantics=("arbitrary",)),
    )(scal, queries, grads, keys, values, *earlier, prefix)
    if shifts:
        return result
    return list(result[:4]) + [None, result[4]]


def shards(
    queries, completion_keys, completion_values, prompt_keys, prompt_values, output_grad, lengths
):
    fsdp = lax.axis_size("fsdp")
    everyone = fsdp * lax.axis_size("sample")
    rows = queries.shape[2]
    keys, values = completion_keys[0, 0], completion_values[0, 0]
    earlier = []
    for s in range(1, fsdp):
        ring = [(i, (i + s) % fsdp) for i in range(fsdp)]
        earlier += [lax.ppermute(keys, "fsdp", ring), lax.ppermute(values, "fsdp", ring)]
    line = jnp.stack([prompt_keys[0], prompt_values[0]], 1).astype(jnp.float32)
    prefix = lax.all_to_all(
        jnp.tile(line, (everyone, 1, 1)),
        ("sample", "fsdp"),
        split_axis=0,
        concat_axis=0,
        tiled=True,
    )
    scal = jnp.stack([lax.axis_index("fsdp"), lengths[0, 0]]).astype(jnp.int32)
    out, dq, dk, dv, dback, dprefix = attend(
        scal, queries[0, 0], output_grad[0, 0], keys, values, earlier, prefix, rows * fsdp
    )
    for s in range(1, fsdp):
        ring = [(i, (i - s) % fsdp) for i in range(fsdp)]
        landed = lax.ppermute(dback[s - 1], "fsdp", ring).astype(jnp.float32)
        dk, dv = dk + landed[0], dv + landed[1]
    shares = lax.all_to_all(dprefix, ("sample", "fsdp"), split_axis=0, concat_axis=0, tiled=True)
    total = jnp.sum(shares.reshape((everyone, -1) + shares.shape[1:]), 0)
    return (
        out[None, None],
        dq[None, None],
        dk[None, None],
        dv[None, None],
        total[None, :, 0],
        total[None, :, 1],
    )


def solution(mesh):
    wide = P(("groups", "prompt"), "sample", "fsdp", None)
    lead = P(("groups", "prompt"), ("sample", "fsdp"), None)
    in_specs = (wide, wide, wide, lead, lead, wide, P(("groups", "prompt"), "sample"))
    out_specs = (wide, wide, wide, wide, lead, lead)
    return jax.shard_map(shards, mesh=mesh, in_specs=in_specs, out_specs=out_specs, check_vma=False)
```

```python
import functools

import jax
import jax.numpy as jnp
from jax import lax
from jax.experimental import pallas as pl
from jax.experimental.pallas import tpu as pltpu
from jax.sharding import PartitionSpec as P

HEAD_DIM = 128
LOG2E = 1.4426950408889634
UNITS = 2
VMEM_LIMIT = 24 << 20

NT = (((1,), (1,)), ((), ()))
NN = (((1,), (0,)), ((), ()))


def mm(a, b, dims=NN):
    return lax.dot_general(a, b, dims, preferred_element_type=jnp.float32)


def pad_rows(x, rows):
    if x.shape[0] == rows:
        return x
    return jnp.concatenate([x, jnp.zeros((rows - x.shape[0], x.shape[1]), x.dtype)], 0)


def attend_kernel(shifts, share, comp_span, scal, q_ref, g_ref, k_ref, v_ref, *refs):
    earlier = refs[: 2 * shifts]
    prefix, out, dq, dk, dv = refs[2 * shifts : 2 * shifts + 5]
    rest = refs[2 * shifts + 5 :]
    dback = rest[0] if shifts else None
    dprefix = rest[-1]
    rows = q_ref.shape[0]
    prompt = prefix.shape[0]
    padded = -(-prompt // 16) * 16
    before = padded + shifts * rows
    chunk = min(rows, 256 // share)
    steps = rows // chunk
    place, length = scal[0], scal[1]
    scale = HEAD_DIM ** -0.5
    factor = scale * LOG2E
    neg = jnp.float32(-jnp.inf)

    units = k_ref.shape[1] // HEAD_DIM
    sides = []
    for u in range(units):
        col = slice(u * HEAD_DIM, (u + 1) * HEAD_DIM)
        lead_k = pad_rows(prefix[:, 0, col], padded).astype(jnp.bfloat16)
        lead_v = pad_rows(prefix[:, 1, col], padded).astype(jnp.bfloat16)
        keys = jnp.concatenate(
            [lead_k] + [earlier[2 * s][:, col] for s in range(shifts)] + [k_ref[:, col]], 0
        )
        values = jnp.concatenate(
            [lead_v] + [earlier[2 * s + 1][:, col] for s in range(shifts)] + [v_ref[:, col]], 0
        )
        sides.append((keys, values, keys.T, values.T))
    bias = [jnp.where(place >= s + 1, jnp.float32(0.0), neg) for s in range(shifts)]
    causal = lax.broadcasted_iota(jnp.int32, (chunk, share * chunk), 0) <= lax.rem(
        lax.broadcasted_iota(jnp.int32, (chunk, share * chunk), 1), chunk
    )
    ratio = jnp.float32(comp_span) / length.astype(jnp.float32)
    heads = [
        [slice((u * share + h) * HEAD_DIM, (u * share + h + 1) * HEAD_DIM) for h in range(share)]
        for u in range(units)
    ]

    def first(u, i):
        keys, values = sides[u][:2]
        head = heads[u]
        part = slice(i * chunk, (i + 1) * chunk)
        token = place * rows + i * chunk + lax.broadcasted_iota(jnp.int32, (chunk, HEAD_DIM), 0)
        weight = jnp.where(token < length, ratio, jnp.float32(0.0))
        q = jnp.concatenate([q_ref[part, c] for c in head], 0)
        g = jnp.concatenate(
            [(g_ref[part, c].astype(jnp.float32) * weight).astype(jnp.bfloat16) for c in head], 0
        )
        seen = before + (i + 1) * chunk
        return q, g, mm(keys[:seen], q, NT), mm(values[:seen], g, NT)

    def second(i, scores, dprob):
        seen = before + (i + 1) * chunk
        lead = scores[:prompt]
        back = [scores[padded + s * rows : padded + (s + 1) * rows] for s in range(shifts)]
        full = scores[before : seen - chunk]
        last = jnp.where(causal, scores[seen - chunk :], neg)
        top = jnp.maximum(jnp.max(last, 0, keepdims=True), jnp.max(lead, 0, keepdims=True))
        if i:
            top = jnp.maximum(top, jnp.max(full, 0, keepdims=True))
        for s in range(shifts):
            top = jnp.maximum(top, jnp.max(back[s], 0, keepdims=True) + bias[s])
        top = top * factor
        parts = [jnp.exp2(lead * factor - top)]
        if padded != prompt:
            parts.append(jnp.zeros((padded - prompt, lead.shape[1]), jnp.float32))
        parts += [jnp.exp2(back[s] * factor - (top - bias[s])) for s in range(shifts)]
        if i:
            parts.append(jnp.exp2(full * factor - top))
        parts.append(jnp.exp2(last * factor - top))
        expo = jnp.concatenate(parts, 0)
        inverse = 1.0 / jnp.sum(expo, 0, keepdims=True)
        dot = jnp.sum(expo * dprob, 0, keepdims=True) * inverse
        probs = expo * inverse
        sgrad = (probs * (dprob - dot)).astype(jnp.bfloat16)
        return probs.astype(jnp.bfloat16), sgrad

    def deep(left, right):
        total = None
        for at in range(0, right.shape[0], 256):
            end = min(at + 256, right.shape[0])
            term = mm(left[:, at:end], right[at:end])
            total = term if total is None else total + term
        return total

    def third(u, i, q, g, probs, sgrad, acc):
        keys_t, values_t = sides[u][2:]
        head = heads[u]
        seen = before + (i + 1) * chunk
        part = slice(i * chunk, (i + 1) * chunk)
        mixed = deep(values_t[:, :seen], probs).astype(jnp.bfloat16).T
        dquery = (deep(keys_t[:, :seen], sgrad) * scale).astype(jnp.bfloat16).T
        for h, c in enumerate(head):
            out[part, c] = mixed[h * chunk : (h + 1) * chunk]
            dq[part, c] = dquery[h * chunk : (h + 1) * chunk]
        new = mm(sgrad, q), mm(probs, g)
        if acc is None:
            return new
        old = acc[0].shape[0]
        return tuple(jnp.concatenate([a + n[:old], n[old:]], 0) for a, n in zip(acc, new))

    def finish(u, acc):
        col = slice(u * HEAD_DIM, (u + 1) * HEAD_DIM)
        key_term, value_term = acc[0] * scale, acc[1]
        dk[:, col] = key_term[before:]
        dv[:, col] = value_term[before:]
        for s in range(shifts):
            at = slice(padded + s * rows, padded + (s + 1) * rows)
            dback[s, 0, :, col] = key_term[at].astype(jnp.bfloat16)
            dback[s, 1, :, col] = value_term[at].astype(jnp.bfloat16)
        dprefix[:, 0, col] = key_term[:prompt]
        dprefix[:, 1, col] = value_term[:prompt]

    order = [(u, i) for u in range(units) for i in range(steps)]
    acc = [None] * units

    def close(work):
        u, i = work[:2]
        acc[u] = third(*work, acc[u])
        if i == steps - 1:
            finish(u, acc[u])

    ahead, behind = first(*order[0]), None
    for n, (u, i) in enumerate(order):
        q, g, scores, dprob = ahead
        if n + 1 < len(order):
            ahead = first(*order[n + 1])
        if behind is not None:
            close(behind)
        probs, sgrad = second(i, scores, dprob)
        behind = (u, i, q, g, probs, sgrad)
    close(behind)


def attend(scal, queries, grads, keys, values, earlier, prefix, comp_span):
    rows, width = queries.shape
    groups = keys.shape[1] // HEAD_DIM
    share = width // HEAD_DIM // groups
    units = UNITS if groups % UNITS == 0 else 1
    shifts = len(earlier) // 2
    prompt = prefix.shape[0]
    wide = pl.BlockSpec((rows, units * share * HEAD_DIM), lambda i, s: (0, i))
    narrow = pl.BlockSpec((rows, units * HEAD_DIM), lambda i, s: (0, i))
    lead = pl.BlockSpec((prompt, 2, units * HEAD_DIM), lambda i, s: (0, 0, i))
    outs = [
        jax.ShapeDtypeStruct((rows, width), jnp.bfloat16),
        jax.ShapeDtypeStruct((rows, width), jnp.bfloat16),
        jax.ShapeDtypeStruct(keys.shape, jnp.float32),
        jax.ShapeDtypeStruct(keys.shape, jnp.float32),
    ]
    out_specs = [wide, wide, narrow, narrow]
    if shifts:
        outs.append(jax.ShapeDtypeStruct((shifts, 2) + keys.shape, jnp.bfloat16))
        out_specs.append(pl.BlockSpec((shifts, 2, rows, units * HEAD_DIM), lambda i, s: (0, 0, 0, i)))
    outs.append(jax.ShapeDtypeStruct(prefix.shape, jnp.float32))
    out_specs.append(lead)
    result = pl.pallas_call(
        functools.partial(attend_kernel, shifts, share, comp_span),
        out_shape=outs,
        grid_spec=pltpu.PrefetchScalarGridSpec(
            num_scalar_prefetch=1,
            grid=(groups // units,),
            in_specs=[wide, wide, narrow, narrow] + [narrow] * (2 * shifts) + [lead],
            out_specs=out_specs,
        ),
        compiler_params=pltpu.CompilerParams(
            dimension_semantics=("arbitrary",), vmem_limit_bytes=VMEM_LIMIT
        ),
    )(scal, queries, grads, keys, values, *earlier, prefix)
    if shifts:
        return result
    return list(result[:4]) + [None, result[4]]


def shards(
    queries, completion_keys, completion_values, prompt_keys, prompt_values, output_grad, lengths
):
    fsdp = lax.axis_size("fsdp")
    everyone = fsdp * lax.axis_size("sample")
    rows = queries.shape[2]
    keys, values = completion_keys[0, 0], completion_values[0, 0]
    earlier = []
    for s in range(1, fsdp):
        ring = [(i, (i + s) % fsdp) for i in range(fsdp)]
        earlier += [lax.ppermute(keys, "fsdp", ring), lax.ppermute(values, "fsdp", ring)]
    line = jnp.stack([prompt_keys[0], prompt_values[0]], 1).astype(jnp.float32)
    prefix = lax.all_to_all(
        jnp.tile(line, (everyone, 1, 1)),
        ("sample", "fsdp"),
        split_axis=0,
        concat_axis=0,
        tiled=True,
    )
    scal = jnp.stack([lax.axis_index("fsdp"), lengths[0, 0]]).astype(jnp.int32)
    out, dq, dk, dv, dback, dprefix = attend(
        scal, queries[0, 0], output_grad[0, 0], keys, values, earlier, prefix, rows * fsdp
    )
    for s in range(1, fsdp):
        ring = [(i, (i - s) % fsdp) for i in range(fsdp)]
        landed = lax.ppermute(dback[s - 1], "fsdp", ring).astype(jnp.float32)
        dk, dv = dk + landed[0], dv + landed[1]
    shares = lax.all_to_all(dprefix, ("sample", "fsdp"), split_axis=0, concat_axis=0, tiled=True)
    total = jnp.sum(shares.reshape((everyone, -1) + shares.shape[1:]), 0)
    return (
        out[None, None],
        dq[None, None],
        dk[None, None],
        dv[None, None],
        total[None, :, 0],
        total[None, :, 1],
    )


def solution(mesh):
    wide = P(("groups", "prompt"), "sample", "fsdp", None)
    lead = P(("groups", "prompt"), ("sample", "fsdp"), None)
    in_specs = (wide, wide, wide, lead, lead, wide, P(("groups", "prompt"), "sample"))
    out_specs = (wide, wide, wide, wide, lead, lead)
    return jax.shard_map(shards, mesh=mesh, in_specs=in_specs, out_specs=out_specs, check_vma=False)
```

```python
import functools

import jax
import jax.numpy as jnp
from jax import lax
from jax.experimental import pallas as pl
from jax.experimental.pallas import tpu as pltpu
from jax.sharding import PartitionSpec as P

HEAD_DIM = 128
LOG2E = 1.4426950408889634
UNITS = 2
PARTS = 4
VMEM_LIMIT = 24 << 20

NT = (((1,), (1,)), ((), ()))
NN = (((1,), (0,)), ((), ()))


def mm(a, b, dims=NN):
    return lax.dot_general(a, b, dims, preferred_element_type=jnp.float32)


def pad_rows(x, rows):
    if x.shape[0] == rows:
        return x
    return jnp.concatenate([x, jnp.zeros((rows - x.shape[0], x.shape[1]), x.dtype)], 0)


def attend_kernel(shifts, share, scal, q_ref, g_ref, k_ref, v_ref, *refs):
    earlier = refs[: 2 * shifts]
    prefix, out, dq, dk, dv = refs[2 * shifts : 2 * shifts + 5]
    rest = refs[2 * shifts + 5 :]
    dback = rest[0] if shifts else None
    dprefix = rest[-1]
    rows = q_ref.shape[0]
    prompt = prefix.shape[0]
    padded = -(-prompt // 16) * 16
    before = padded + shifts * rows
    chunk = min(rows, 256 // share)
    steps = rows // chunk
    place = scal[0]
    scale = HEAD_DIM ** -0.5
    factor = scale * LOG2E
    neg = jnp.float32(-jnp.inf)

    units = k_ref.shape[1] // HEAD_DIM
    sides = []
    for u in range(units):
        col = slice(u * HEAD_DIM, (u + 1) * HEAD_DIM)
        lead_k = pad_rows(prefix[:, 0, col], padded).astype(jnp.bfloat16)
        lead_v = pad_rows(prefix[:, 1, col], padded).astype(jnp.bfloat16)
        keys = jnp.concatenate(
            [lead_k] + [earlier[2 * s][:, col] for s in range(shifts)] + [k_ref[:, col]], 0
        )
        values = jnp.concatenate(
            [lead_v] + [earlier[2 * s + 1][:, col] for s in range(shifts)] + [v_ref[:, col]], 0
        )
        sides.append((keys, values, keys.T, values.T))
    bias = [jnp.where(place >= s + 1, jnp.float32(0.0), neg) for s in range(shifts)]
    causal = lax.broadcasted_iota(jnp.int32, (chunk, share * chunk), 0) <= lax.rem(
        lax.broadcasted_iota(jnp.int32, (chunk, share * chunk), 1), chunk
    )
    heads = [
        [slice((u * share + h) * HEAD_DIM, (u * share + h + 1) * HEAD_DIM) for h in range(share)]
        for u in range(units)
    ]

    def first(u, i):
        keys, values = sides[u][:2]
        head = heads[u]
        part = slice(i * chunk, (i + 1) * chunk)
        q = jnp.concatenate([q_ref[part, c] for c in head], 0)
        g = jnp.concatenate([g_ref[part, c] for c in head], 0)
        seen = before + (i + 1) * chunk
        return q, g, mm(keys[:seen], q, NT), mm(values[:seen], g, NT)

    def second(i, scores, dprob):
        seen = before + (i + 1) * chunk
        lead = scores[:prompt]
        back = [scores[padded + s * rows : padded + (s + 1) * rows] for s in range(shifts)]
        full = scores[before : seen - chunk]
        last = jnp.where(causal, scores[seen - chunk :], neg)
        top = jnp.maximum(jnp.max(last, 0, keepdims=True), jnp.max(lead, 0, keepdims=True))
        if i:
            top = jnp.maximum(top, jnp.max(full, 0, keepdims=True))
        for s in range(shifts):
            top = jnp.maximum(top, jnp.max(back[s], 0, keepdims=True) + bias[s])
        top = top * factor
        parts = [jnp.exp2(lead * factor - top)]
        if padded != prompt:
            parts.append(jnp.zeros((padded - prompt, lead.shape[1]), jnp.float32))
        parts += [jnp.exp2(back[s] * factor - (top - bias[s])) for s in range(shifts)]
        if i:
            parts.append(jnp.exp2(full * factor - top))
        parts.append(jnp.exp2(last * factor - top))
        expo = jnp.concatenate(parts, 0)
        inverse = 1.0 / jnp.sum(expo, 0, keepdims=True)
        dot = jnp.sum(expo * dprob, 0, keepdims=True) * inverse
        probs = expo * inverse
        sgrad = (probs * (dprob - dot)).astype(jnp.bfloat16)
        return probs.astype(jnp.bfloat16), sgrad

    def deep(left, right):
        total = None
        for at in range(0, right.shape[0], 256):
            end = min(at + 256, right.shape[0])
            term = mm(left[:, at:end], right[at:end])
            total = term if total is None else total + term
        return total

    def third(u, i, q, g, probs, sgrad, acc):
        keys_t, values_t = sides[u][2:]
        head = heads[u]
        seen = before + (i + 1) * chunk
        part = slice(i * chunk, (i + 1) * chunk)
        mixed = deep(values_t[:, :seen], probs).astype(jnp.bfloat16).T
        dquery = (deep(keys_t[:, :seen], sgrad) * scale).astype(jnp.bfloat16).T
        for h, c in enumerate(head):
            out[part, c] = mixed[h * chunk : (h + 1) * chunk]
            dq[part, c] = dquery[h * chunk : (h + 1) * chunk]
        new = mm(sgrad, q), mm(probs, g)
        if acc is None:
            return new
        old = acc[0].shape[0]
        return tuple(jnp.concatenate([a + n[:old], n[old:]], 0) for a, n in zip(acc, new))

    def finish(u, acc):
        col = slice(u * HEAD_DIM, (u + 1) * HEAD_DIM)
        key_term, value_term = acc[0] * scale, acc[1]
        dk[:, col] = key_term[before:]
        dv[:, col] = value_term[before:]
        for s in range(shifts):
            at = slice(padded + s * rows, padded + (s + 1) * rows)
            dback[s, 0, :, col] = key_term[at].astype(jnp.bfloat16)
            dback[s, 1, :, col] = value_term[at].astype(jnp.bfloat16)
        dprefix[:, 0, col] = key_term[:prompt]
        dprefix[:, 1, col] = value_term[:prompt]

    order = [(u, i) for u in range(units) for i in range(steps)]
    acc = [None] * units

    def close(work):
        u, i = work[:2]
        acc[u] = third(*work, acc[u])
        if i == steps - 1:
            finish(u, acc[u])

    ahead, behind = first(*order[0]), None
    for n, (u, i) in enumerate(order):
        q, g, scores, dprob = ahead
        if n + 1 < len(order):
            ahead = first(*order[n + 1])
        if behind is not None:
            close(behind)
        probs, sgrad = second(i, scores, dprob)
        behind = (u, i, q, g, probs, sgrad)
    close(behind)


def attend(scal, queries, grads, keys, values, earlier, prefix):
    rows, width = queries.shape
    groups = keys.shape[1] // HEAD_DIM
    share = width // HEAD_DIM // groups
    units = UNITS if groups % UNITS == 0 else 1
    shifts = len(earlier) // 2
    prompt = prefix.shape[0]
    wide = pl.BlockSpec((rows, units * share * HEAD_DIM), lambda i, s: (0, i))
    narrow = pl.BlockSpec((rows, units * HEAD_DIM), lambda i, s: (0, i))
    lead = pl.BlockSpec((prompt, 2, units * HEAD_DIM), lambda i, s: (0, 0, i))
    outs = [
        jax.ShapeDtypeStruct((rows, width), jnp.bfloat16),
        jax.ShapeDtypeStruct((rows, width), jnp.bfloat16),
        jax.ShapeDtypeStruct(keys.shape, jnp.float32),
        jax.ShapeDtypeStruct(keys.shape, jnp.float32),
    ]
    out_specs = [wide, wide, narrow, narrow]
    if shifts:
        outs.append(jax.ShapeDtypeStruct((shifts, 2) + keys.shape, jnp.bfloat16))
        out_specs.append(pl.BlockSpec((shifts, 2, rows, units * HEAD_DIM), lambda i, s: (0, 0, 0, i)))
    outs.append(jax.ShapeDtypeStruct(prefix.shape, jnp.float32))
    out_specs.append(lead)
    result = pl.pallas_call(
        functools.partial(attend_kernel, shifts, share),
        out_shape=outs,
        grid_spec=pltpu.PrefetchScalarGridSpec(
            num_scalar_prefetch=1,
            grid=(groups // units,),
            in_specs=[wide, wide, narrow, narrow] + [narrow] * (2 * shifts) + [lead],
            out_specs=out_specs,
        ),
        compiler_params=pltpu.CompilerParams(
            dimension_semantics=("arbitrary",), vmem_limit_bytes=VMEM_LIMIT
        ),
    )(scal, queries, grads, keys, values, *earlier, prefix)
    if shifts:
        return result
    return list(result[:4]) + [None, result[4]]


def prepare_kernel(comp_span, scal, q_ref, g_ref, k_ref, v_ref, q_out, g_out, k_out, v_out):
    rows, width = g_ref.shape
    place, length = scal[0], scal[1]
    ratio = jnp.float32(comp_span) / length.astype(jnp.float32)
    token = place * rows + lax.broadcasted_iota(jnp.int32, (rows, HEAD_DIM), 0)
    weight = jnp.where(token < length, ratio, jnp.float32(0.0))
    for at in range(0, width, HEAD_DIM):
        c = slice(at, at + HEAD_DIM)
        g_out[:, c] = (g_ref[:, c].astype(jnp.float32) * weight).astype(jnp.bfloat16)
    q_out[...] = q_ref[...]
    k_out[...] = k_ref[...]
    v_out[...] = v_ref[...]


def prepare(scal, queries, grads, keys, values, comp_span):
    rows, width = queries.shape
    parts = PARTS if width % (PARTS * HEAD_DIM) == 0 and keys.shape[1] % (PARTS * HEAD_DIM) == 0 else 1
    wide = pl.BlockSpec((rows, width // parts), lambda i, s: (0, i))
    narrow = pl.BlockSpec((rows, keys.shape[1] // parts), lambda i, s: (0, i))
    specs = [wide, wide, narrow, narrow]
    moved = 2 * 2 * (queries.size + grads.size + keys.size + values.size)
    return pl.pallas_call(
        functools.partial(prepare_kernel, comp_span),
        out_shape=[jax.ShapeDtypeStruct(x.shape, x.dtype) for x in (queries, grads, keys, values)],
        grid_spec=pltpu.PrefetchScalarGridSpec(
            num_scalar_prefetch=1, grid=(parts,), in_specs=specs, out_specs=specs
        ),
        cost_estimate=pl.CostEstimate(flops=grads.size, bytes_accessed=moved, transcendentals=0),
        compiler_params=pltpu.CompilerParams(
            dimension_semantics=("arbitrary",), vmem_limit_bytes=VMEM_LIMIT
        ),
    )(scal, *(pltpu.with_memory_space_constraint(x, pltpu.HBM) for x in (queries, grads, keys, values)))


def shards(
    queries, completion_keys, completion_values, prompt_keys, prompt_values, output_grad, lengths
):
    fsdp = lax.axis_size("fsdp")
    everyone = fsdp * lax.axis_size("sample")
    rows = queries.shape[2]
    keys, values = completion_keys[0, 0], completion_values[0, 0]
    earlier = []
    for s in range(1, fsdp):
        ring = [(i, (i + s) % fsdp) for i in range(fsdp)]
        earlier += [lax.ppermute(keys, "fsdp", ring), lax.ppermute(values, "fsdp", ring)]
    line = jnp.stack([prompt_keys[0], prompt_values[0]], 1).astype(jnp.float32)
    prefix = lax.all_to_all(
        jnp.tile(line, (everyone, 1, 1)),
        ("sample", "fsdp"),
        split_axis=0,
        concat_axis=0,
        tiled=True,
    )
    scal = jnp.stack([lax.axis_index("fsdp"), lengths[0, 0]]).astype(jnp.int32)
    with jax.named_scope("prepare"):
        q, g, k, v = prepare(
            scal, queries[0, 0], output_grad[0, 0], keys, values, rows * fsdp
        )
    with jax.named_scope("attend"):
        out, dq, dk, dv, dback, dprefix = attend(scal, q, g, k, v, earlier, prefix)
    for s in range(1, fsdp):
        ring = [(i, (i - s) % fsdp) for i in range(fsdp)]
        landed = lax.ppermute(dback[s - 1], "fsdp", ring).astype(jnp.float32)
        dk, dv = dk + landed[0], dv + landed[1]
    shares = lax.all_to_all(dprefix, ("sample", "fsdp"), split_axis=0, concat_axis=0, tiled=True)
    total = jnp.sum(shares.reshape((everyone, -1) + shares.shape[1:]), 0)
    return (
        out[None, None],
        dq[None, None],
        dk[None, None],
        dv[None, None],
        total[None, :, 0],
        total[None, :, 1],
    )


def solution(mesh):
    wide = P(("groups", "prompt"), "sample", "fsdp", None)
    lead = P(("groups", "prompt"), ("sample", "fsdp"), None)
    in_specs = (wide, wide, wide, lead, lead, wide, P(("groups", "prompt"), "sample"))
    out_specs = (wide, wide, wide, wide, lead, lead)
    return jax.shard_map(shards, mesh=mesh, in_specs=in_specs, out_specs=out_specs, check_vma=False)
```

```python
import functools

import jax
import jax.numpy as jnp
from jax import lax
from jax.experimental import pallas as pl
from jax.experimental.pallas import tpu as pltpu
from jax.sharding import PartitionSpec as P

HEAD_DIM = 128
LOG2E = 1.4426950408889634
UNITS = 2
PARTS = 4
VMEM_LIMIT = 24 << 20

NT = (((1,), (1,)), ((), ()))
NN = (((1,), (0,)), ((), ()))


def mm(a, b, dims=NN):
    return lax.dot_general(a, b, dims, preferred_element_type=jnp.float32)


def pad_rows(x, rows):
    if x.shape[0] == rows:
        return x
    return jnp.concatenate([x, jnp.zeros((rows - x.shape[0], x.shape[1]), x.dtype)], 0)


def attend_kernel(shifts, share, q_ref, g_ref, k_ref, v_ref, *refs):
    earlier = refs[: 2 * shifts]
    prefix, out, dq, dk, dv = refs[2 * shifts : 2 * shifts + 5]
    rest = refs[2 * shifts + 5 :]
    dback = rest[0] if shifts else None
    dprefix = rest[-1]
    rows = q_ref.shape[0]
    prompt = prefix.shape[0]
    padded = -(-prompt // 16) * 16
    before = padded + shifts * rows
    chunk = min(rows, 256 // share)
    steps = rows // chunk
    place = lax.axis_index("fsdp")
    scale = HEAD_DIM ** -0.5
    factor = scale * LOG2E
    neg = jnp.float32(-jnp.inf)

    units = k_ref.shape[1] // HEAD_DIM
    sides = []
    for u in range(units):
        col = slice(u * HEAD_DIM, (u + 1) * HEAD_DIM)
        lead_k = pad_rows(prefix[:, 0, col], padded).astype(jnp.bfloat16)
        lead_v = pad_rows(prefix[:, 1, col], padded).astype(jnp.bfloat16)
        keys = jnp.concatenate(
            [lead_k] + [earlier[2 * s][:, col] for s in range(shifts)] + [k_ref[:, col]], 0
        )
        values = jnp.concatenate(
            [lead_v] + [earlier[2 * s + 1][:, col] for s in range(shifts)] + [v_ref[:, col]], 0
        )
        sides.append((keys, values, keys.T, values.T))
    bias = [jnp.where(place >= s + 1, jnp.float32(0.0), neg) for s in range(shifts)]
    causal = lax.broadcasted_iota(jnp.int32, (chunk, share * chunk), 0) <= lax.rem(
        lax.broadcasted_iota(jnp.int32, (chunk, share * chunk), 1), chunk
    )
    heads = [
        [slice((u * share + h) * HEAD_DIM, (u * share + h + 1) * HEAD_DIM) for h in range(share)]
        for u in range(units)
    ]

    def first(u, i):
        keys, values = sides[u][:2]
        head = heads[u]
        part = slice(i * chunk, (i + 1) * chunk)
        q = jnp.concatenate([q_ref[part, c] for c in head], 0)
        g = jnp.concatenate([g_ref[part, c] for c in head], 0)
        seen = before + (i + 1) * chunk
        return q, g, mm(keys[:seen], q, NT), mm(values[:seen], g, NT)

    def second(i, scores, dprob):
        seen = before + (i + 1) * chunk
        lead = scores[:prompt]
        back = [scores[padded + s * rows : padded + (s + 1) * rows] for s in range(shifts)]
        full = scores[before : seen - chunk]
        last = jnp.where(causal, scores[seen - chunk :], neg)
        top = jnp.maximum(jnp.max(last, 0, keepdims=True), jnp.max(lead, 0, keepdims=True))
        if i:
            top = jnp.maximum(top, jnp.max(full, 0, keepdims=True))
        for s in range(shifts):
            top = jnp.maximum(top, jnp.max(back[s], 0, keepdims=True) + bias[s])
        top = top * factor
        parts = [jnp.exp2(lead * factor - top)]
        if padded != prompt:
            parts.append(jnp.zeros((padded - prompt, lead.shape[1]), jnp.float32))
        parts += [jnp.exp2(back[s] * factor - (top - bias[s])) for s in range(shifts)]
        if i:
            parts.append(jnp.exp2(full * factor - top))
        parts.append(jnp.exp2(last * factor - top))
        expo = jnp.concatenate(parts, 0)
        inverse = 1.0 / jnp.sum(expo, 0, keepdims=True)
        dot = jnp.sum(expo * dprob, 0, keepdims=True) * inverse
        probs = expo * inverse
        sgrad = (probs * (dprob - dot)).astype(jnp.bfloat16)
        return probs.astype(jnp.bfloat16), sgrad

    def deep(left, right):
        total = None
        for at in range(0, right.shape[0], 256):
            end = min(at + 256, right.shape[0])
            term = mm(left[:, at:end], right[at:end])
            total = term if total is None else total + term
        return total

    def third(u, i, q, g, probs, sgrad, acc):
        keys_t, values_t = sides[u][2:]
        head = heads[u]
        seen = before + (i + 1) * chunk
        part = slice(i * chunk, (i + 1) * chunk)
        mixed = deep(values_t[:, :seen], probs).astype(jnp.bfloat16).T
        dquery = (deep(keys_t[:, :seen], sgrad) * scale).astype(jnp.bfloat16).T
        for h, c in enumerate(head):
            out[part, c] = mixed[h * chunk : (h + 1) * chunk]
            dq[part, c] = dquery[h * chunk : (h + 1) * chunk]
        new = mm(sgrad, q), mm(probs, g)
        if acc is None:
            return new
        old = acc[0].shape[0]
        return tuple(jnp.concatenate([a + n[:old], n[old:]], 0) for a, n in zip(acc, new))

    def finish(u, acc):
        col = slice(u * HEAD_DIM, (u + 1) * HEAD_DIM)
        key_term, value_term = acc[0] * scale, acc[1]
        dk[:, col] = key_term[before:]
        dv[:, col] = value_term[before:]
        for s in range(shifts):
            at = slice(padded + s * rows, padded + (s + 1) * rows)
            dback[s, 0, :, col] = key_term[at].astype(jnp.bfloat16)
            dback[s, 1, :, col] = value_term[at].astype(jnp.bfloat16)
        dprefix[:, 0, col] = key_term[:prompt]
        dprefix[:, 1, col] = value_term[:prompt]

    order = [(u, i) for u in range(units) for i in range(steps)]
    acc = [None] * units

    def close(work):
        u, i = work[:2]
        acc[u] = third(*work, acc[u])
        if i == steps - 1:
            finish(u, acc[u])

    ahead, behind = first(*order[0]), None
    for n, (u, i) in enumerate(order):
        q, g, scores, dprob = ahead
        if n + 1 < len(order):
            ahead = first(*order[n + 1])
        if behind is not None:
            close(behind)
        probs, sgrad = second(i, scores, dprob)
        behind = (u, i, q, g, probs, sgrad)
    close(behind)


def attend(queries, grads, keys, values, earlier, prefix):
    rows, width = queries.shape
    groups = keys.shape[1] // HEAD_DIM
    share = width // HEAD_DIM // groups
    units = UNITS if groups % UNITS == 0 else 1
    shifts = len(earlier) // 2
    prompt = prefix.shape[0]
    wide = pl.BlockSpec((rows, units * share * HEAD_DIM), lambda i: (0, i))
    narrow = pl.BlockSpec((rows, units * HEAD_DIM), lambda i: (0, i))
    lead = pl.BlockSpec((prompt, 2, units * HEAD_DIM), lambda i: (0, 0, i))
    outs = [
        jax.ShapeDtypeStruct((rows, width), jnp.bfloat16),
        jax.ShapeDtypeStruct((rows, width), jnp.bfloat16),
        jax.ShapeDtypeStruct(keys.shape, jnp.float32),
        jax.ShapeDtypeStruct(keys.shape, jnp.float32),
    ]
    out_specs = [wide, wide, narrow, narrow]
    if shifts:
        outs.append(jax.ShapeDtypeStruct((shifts, 2) + keys.shape, jnp.bfloat16))
        out_specs.append(pl.BlockSpec((shifts, 2, rows, units * HEAD_DIM), lambda i: (0, 0, 0, i)))
    outs.append(jax.ShapeDtypeStruct(prefix.shape, jnp.float32))
    out_specs.append(lead)
    result = pl.pallas_call(
        functools.partial(attend_kernel, shifts, share),
        out_shape=outs,
        grid=(groups // units,),
        in_specs=[wide, wide, narrow, narrow] + [narrow] * (2 * shifts) + [lead],
        out_specs=out_specs,
        compiler_params=pltpu.CompilerParams(
            dimension_semantics=("arbitrary",), vmem_limit_bytes=VMEM_LIMIT
        ),
    )(queries, grads, keys, values, *earlier, prefix)
    if shifts:
        return result
    return list(result[:4]) + [None, result[4]]


def prepare_kernel(comp_span, length_ref, g_ref, *refs):
    sources, g_out, targets, sems = refs[:3], refs[3], refs[4:7], refs[7]
    copies = [pltpu.make_async_copy(a, b, sems.at[n]) for n, (a, b) in enumerate(zip(sources, targets))]

    @pl.when(pl.program_id(0) == 0)
    def _():
        for copy in copies:
            copy.start()

    rows, width = g_ref.shape
    length = length_ref[0, 0]
    ratio = jnp.float32(comp_span) / length.astype(jnp.float32)
    token = lax.axis_index("fsdp") * rows + lax.broadcasted_iota(jnp.int32, (rows, HEAD_DIM), 0)
    weight = jnp.where(token < length, ratio, jnp.float32(0.0))
    for at in range(0, width, HEAD_DIM):
        c = slice(at, at + HEAD_DIM)
        g_out[:, c] = (g_ref[:, c].astype(jnp.float32) * weight).astype(jnp.bfloat16)

    @pl.when(pl.program_id(0) == pl.num_programs(0) - 1)
    def _():
        for copy in copies:
            copy.wait()


def prepare(lengths, queries, grads, keys, values, comp_span):
    rows, width = grads.shape
    parts = PARTS if width % (PARTS * HEAD_DIM) == 0 else 1
    wide = pl.BlockSpec((rows, width // parts), lambda i: (0, i))
    whole = pl.BlockSpec(memory_space=pl.ANY)
    arrays = [pltpu.with_memory_space_constraint(x, pltpu.HBM) for x in (grads, queries, keys, values)]
    moved = 2 * 2 * (queries.size + grads.size + keys.size + values.size)
    g, q, k, v = pl.pallas_call(
        functools.partial(prepare_kernel, comp_span),
        out_shape=[jax.ShapeDtypeStruct(x.shape, x.dtype) for x in arrays],
        grid=(parts,),
        in_specs=[pl.BlockSpec(memory_space=pltpu.SMEM), wide, whole, whole, whole],
        out_specs=[wide, whole, whole, whole],
        scratch_shapes=[pltpu.SemaphoreType.DMA((3,))],
        cost_estimate=pl.CostEstimate(flops=grads.size, bytes_accessed=moved, transcendentals=0),
        compiler_params=pltpu.CompilerParams(
            dimension_semantics=("arbitrary",), vmem_limit_bytes=VMEM_LIMIT
        ),
    )(lengths, *arrays)
    return q, g, k, v


def shards(
    queries, completion_keys, completion_values, prompt_keys, prompt_values, output_grad, lengths
):
    fsdp = lax.axis_size("fsdp")
    everyone = fsdp * lax.axis_size("sample")
    rows = queries.shape[2]
    keys, values = completion_keys[0, 0], completion_values[0, 0]
    earlier = []
    for s in range(1, fsdp):
        ring = [(i, (i + s) % fsdp) for i in range(fsdp)]
        earlier += [lax.ppermute(keys, "fsdp", ring), lax.ppermute(values, "fsdp", ring)]
    line = jnp.stack([prompt_keys[0], prompt_values[0]], 1).astype(jnp.float32)
    prefix = lax.all_to_all(
        jnp.tile(line, (everyone, 1, 1)),
        ("sample", "fsdp"),
        split_axis=0,
        concat_axis=0,
        tiled=True,
    )
    q, g, k, v = prepare(lengths, queries[0, 0], output_grad[0, 0], keys, values, rows * fsdp)
    out, dq, dk, dv, dback, dprefix = attend(q, g, k, v, earlier, prefix)
    landed = []
    for s in range(1, fsdp):
        ring = [(i, (i - s) % fsdp) for i in range(fsdp)]
        landed.append(lax.ppermute(dback[s - 1], "fsdp", ring))
    shares = lax.all_to_all(dprefix, ("sample", "fsdp"), split_axis=0, concat_axis=0, tiled=True)
    for block in landed:
        block = block.astype(jnp.float32)
        dk, dv = dk + block[0], dv + block[1]
    total = jnp.sum(shares.reshape((everyone, -1) + shares.shape[1:]), 0)
    return (
        out[None, None],
        dq[None, None],
        dk[None, None],
        dv[None, None],
        total[None, :, 0],
        total[None, :, 1],
    )


def solution(mesh):
    wide = P(("groups", "prompt"), "sample", "fsdp", None)
    lead = P(("groups", "prompt"), ("sample", "fsdp"), None)
    in_specs = (wide, wide, wide, lead, lead, wide, P(("groups", "prompt"), "sample"))
    out_specs = (wide, wide, wide, wide, lead, lead)
    return jax.shard_map(shards, mesh=mesh, in_specs=in_specs, out_specs=out_specs, check_vma=False)
```

```python
import functools

import jax
import jax.numpy as jnp
from jax import lax
from jax.experimental import pallas as pl
from jax.experimental.pallas import tpu as pltpu
from jax.sharding import PartitionSpec as P

HEAD_DIM = 128
LOG2E = 1.4426950408889634
UNITS = 2
PARTS = 4
VMEM_LIMIT = 24 << 20

NT = (((1,), (1,)), ((), ()))
NN = (((1,), (0,)), ((), ()))


def mm(a, b, dims=NN):
    return lax.dot_general(a, b, dims, preferred_element_type=jnp.float32)


def pad_rows(x, rows):
    if x.shape[0] == rows:
        return x
    return jnp.concatenate([x, jnp.zeros((rows - x.shape[0], x.shape[1]), x.dtype)], 0)


def geometry(q_ref, prefix, k_ref, shifts, share):
    rows = q_ref.shape[0]
    prompt = prefix.shape[0]
    padded = -(-prompt // 16) * 16
    chunk = min(rows, 256 // share)
    return rows, prompt, padded, padded + shifts * rows, chunk, k_ref.shape[1] // HEAD_DIM


def sides_of(units, padded, prefix, earlier, k_ref, v_ref):
    sides = []
    for u in range(units):
        col = slice(u * HEAD_DIM, (u + 1) * HEAD_DIM)
        pair = []
        for which, own in enumerate((k_ref, v_ref)):
            lead = pad_rows(prefix[:, which, col], padded).astype(jnp.bfloat16)
            past = [block[:, col] for block in earlier[which::2]]
            pair.append(jnp.concatenate([lead] + past + [own[:, col]], 0))
        sides.append(pair)
    return sides


def stacked(ref, u, share, part):
    return jnp.concatenate(
        [
            ref[part, (u * share + h) * HEAD_DIM : (u * share + h + 1) * HEAD_DIM]
            for h in range(share)
        ],
        0,
    )


def pieces(scores, seen, chunk, rows, prompt, padded, before, shifts):
    lead = scores[:prompt]
    back = [scores[padded + s * rows : padded + (s + 1) * rows] for s in range(shifts)]
    full = scores[before : seen - chunk]
    key = lax.broadcasted_iota(jnp.int32, (chunk, scores.shape[1]), 0)
    token = lax.rem(lax.broadcasted_iota(jnp.int32, (chunk, scores.shape[1]), 1), chunk)
    last = jnp.where(key <= token, scores[seen - chunk :], jnp.float32(-jnp.inf))
    return lead, back, full, last


def exponents(parts, top, bias, factor, padded):
    lead, back, full, last = parts
    out = [jnp.exp2(lead * factor - top)]
    if padded != lead.shape[0]:
        out.append(jnp.zeros((padded - lead.shape[0], lead.shape[1]), jnp.float32))
    out += [jnp.exp2(b * factor - (top - o)) for b, o in zip(back, bias)]
    if full.shape[0]:
        out.append(jnp.exp2(full * factor - top))
    out.append(jnp.exp2(last * factor - top))
    return jnp.concatenate(out, 0)


def biases(shifts):
    place = lax.axis_index("fsdp")
    return [
        jnp.where(place >= s + 1, jnp.float32(0.0), jnp.float32(-jnp.inf)) for s in range(shifts)
    ]


def grown(acc, new):
    if acc is None:
        return new
    old = acc[0].shape[0]
    return tuple(
        jnp.concatenate([a + n[:old], n[old:]], 0) if n.shape[0] > old else a + n
        for a, n in zip(acc, new)
    )


def pipeline(order, first, second, third):
    ahead, behind = first(*order[0]), None
    for n, (u, i) in enumerate(order):
        now = ahead
        if n + 1 < len(order):
            ahead = first(*order[n + 1])
        if behind is not None:
            third(*behind)
        behind = (u, i) + second(u, i, *now)
    third(*behind)


def travel_kernel(shifts, share, q_ref, g_ref, k_ref, v_ref, *refs):
    earlier, prefix = refs[: 2 * shifts], refs[2 * shifts]
    rest = refs[2 * shifts + 1 :]
    dback = rest[0] if shifts else None
    dprefix, stats = rest[-2:]
    rows, prompt, padded, before, chunk, units = geometry(q_ref, prefix, k_ref, shifts, share)
    steps = rows // chunk
    scale = HEAD_DIM ** -0.5
    factor = scale * LOG2E
    bias = biases(shifts)
    sides = sides_of(units, padded, prefix, earlier, k_ref, v_ref)
    acc = [None] * units

    def first(u, i):
        keys, values = sides[u]
        part = slice(i * chunk, (i + 1) * chunk)
        q, g = stacked(q_ref, u, share, part), stacked(g_ref, u, share, part)
        seen = before + (i + 1) * chunk
        return q, g, mm(keys[:seen], q, NT), mm(values[:seen], g, NT)

    def second(u, i, q, g, scores, dprob):
        seen = before + (i + 1) * chunk
        parts = pieces(scores, seen, chunk, rows, prompt, padded, before, shifts)
        lead, back, full, last = parts
        top = jnp.maximum(jnp.max(last, 0, keepdims=True), jnp.max(lead, 0, keepdims=True))
        if i:
            top = jnp.maximum(top, jnp.max(full, 0, keepdims=True))
        for s in range(shifts):
            top = jnp.maximum(top, jnp.max(back[s], 0, keepdims=True) + bias[s])
        top = top * factor
        expo = exponents(parts, top, bias, factor, padded)
        inverse = 1.0 / jnp.sum(expo, 0, keepdims=True)
        dot = jnp.sum(expo * dprob, 0, keepdims=True) * inverse
        n = u * steps + i
        stats[n, 0:1] = top
        stats[n, 1:2] = inverse
        stats[n, 2:3] = dot
        probs = expo[:before] * inverse
        sgrad = (probs * (dprob[:before] - dot)).astype(jnp.bfloat16)
        return q, g, probs.astype(jnp.bfloat16), sgrad

    def third(u, i, q, g, probs, sgrad):
        acc[u] = grown(acc[u], (mm(sgrad, q), mm(probs, g)))
        if i < steps - 1:
            return
        col = slice(u * HEAD_DIM, (u + 1) * HEAD_DIM)
        key_term, value_term = acc[u][0] * scale, acc[u][1]
        for s in range(shifts):
            at = slice(padded + s * rows, padded + (s + 1) * rows)
            dback[s, 0, :, col] = key_term[at].astype(jnp.bfloat16)
            dback[s, 1, :, col] = value_term[at].astype(jnp.bfloat16)
        dprefix[:, 0, col] = key_term[:prompt]
        dprefix[:, 1, col] = value_term[:prompt]

    pipeline([(u, i) for u in range(units) for i in range(steps)], first, second, third)


def stay_kernel(shifts, share, q_ref, g_ref, k_ref, v_ref, *refs):
    earlier, prefix, stats = refs[: 2 * shifts], refs[2 * shifts], refs[2 * shifts + 1]
    out, dq, dk, dv = refs[2 * shifts + 2 :]
    rows, prompt, padded, before, chunk, units = geometry(q_ref, prefix, k_ref, shifts, share)
    steps = rows // chunk
    scale = HEAD_DIM ** -0.5
    factor = scale * LOG2E
    bias = biases(shifts)
    sides = [
        (keys, values, keys.T, values.T)
        for keys, values in sides_of(units, padded, prefix, earlier, k_ref, v_ref)
    ]
    acc = [None] * units

    def first(u, i):
        keys, values = sides[u][:2]
        part = slice(i * chunk, (i + 1) * chunk)
        q, g = stacked(q_ref, u, share, part), stacked(g_ref, u, share, part)
        seen = before + (i + 1) * chunk
        return q, g, mm(keys[:seen], q, NT), mm(values[:seen], g, NT)

    def second(u, i, q, g, scores, dprob):
        seen = before + (i + 1) * chunk
        n = u * steps + i
        top, inverse, dot = stats[n, 0:1], stats[n, 1:2], stats[n, 2:3]
        parts = pieces(scores, seen, chunk, rows, prompt, padded, before, shifts)
        probs = exponents(parts, top, bias, factor, padded) * inverse
        sgrad = (probs * (dprob - dot)).astype(jnp.bfloat16)
        return q, g, probs.astype(jnp.bfloat16), sgrad

    def deep(left, right):
        total = None
        for at in range(0, right.shape[0], 256):
            end = min(at + 256, right.shape[0])
            term = mm(left[:, at:end], right[at:end])
            total = term if total is None else total + term
        return total

    def third(u, i, q, g, probs, sgrad):
        keys_t, values_t = sides[u][2:]
        seen = before + (i + 1) * chunk
        part = slice(i * chunk, (i + 1) * chunk)
        mixed = deep(values_t[:, :seen], probs).astype(jnp.bfloat16).T
        dquery = (deep(keys_t[:, :seen], sgrad) * scale).astype(jnp.bfloat16).T
        for h in range(share):
            c = slice((u * share + h) * HEAD_DIM, (u * share + h + 1) * HEAD_DIM)
            out[part, c] = mixed[h * chunk : (h + 1) * chunk]
            dq[part, c] = dquery[h * chunk : (h + 1) * chunk]
        acc[u] = grown(acc[u], (mm(sgrad[before:], q), mm(probs[before:], g)))
        if i == steps - 1:
            col = slice(u * HEAD_DIM, (u + 1) * HEAD_DIM)
            dk[:, col] = acc[u][0] * scale
            dv[:, col] = acc[u][1]

    pipeline([(u, i) for u in range(units) for i in range(steps)], first, second, third)


def specs_of(queries, keys, prefix):
    rows, width = queries.shape
    groups = keys.shape[1] // HEAD_DIM
    share = width // HEAD_DIM // groups
    units = UNITS if groups % UNITS == 0 else 1
    chunks = rows // min(rows, 256 // share)
    columns = share * rows // chunks
    wide = pl.BlockSpec((rows, units * share * HEAD_DIM), lambda i: (0, i))
    narrow = pl.BlockSpec((rows, units * HEAD_DIM), lambda i: (0, i))
    lead = pl.BlockSpec((prefix.shape[0], 2, units * HEAD_DIM), lambda i: (0, 0, i))
    stats = pl.BlockSpec((units * chunks, 8, columns), lambda i: (i, 0, 0))
    stats_shape = jax.ShapeDtypeStruct((groups * chunks, 8, columns), jnp.float32)
    return groups // units, units, share, wide, narrow, lead, stats, stats_shape


def travel(queries, grads, keys, values, earlier, prefix):
    steps, units, share, wide, narrow, lead, stats, stats_shape = specs_of(queries, keys, prefix)
    rows = queries.shape[0]
    shifts = len(earlier) // 2
    outs, out_specs = [], []
    if shifts:
        outs.append(jax.ShapeDtypeStruct((shifts, 2) + keys.shape, jnp.bfloat16))
        out_specs.append(pl.BlockSpec((shifts, 2, rows, units * HEAD_DIM), lambda i: (0, 0, 0, i)))
    outs += [jax.ShapeDtypeStruct(prefix.shape, jnp.float32), stats_shape]
    out_specs += [lead, stats]
    result = pl.pallas_call(
        functools.partial(travel_kernel, shifts, share),
        out_shape=outs,
        grid=(steps,),
        in_specs=[wide, wide, narrow, narrow] + [narrow] * (2 * shifts) + [lead],
        out_specs=out_specs,
        compiler_params=pltpu.CompilerParams(
            dimension_semantics=("arbitrary",), vmem_limit_bytes=VMEM_LIMIT
        ),
    )(queries, grads, keys, values, *earlier, prefix)
    return result if shifts else [None] + list(result)


def stay(queries, grads, keys, values, earlier, prefix, marks):
    steps, _, share, wide, narrow, lead, stats, _ = specs_of(queries, keys, prefix)
    shifts = len(earlier) // 2
    total = keys.shape[0] * (1 + shifts) + prefix.shape[0]
    return pl.pallas_call(
        functools.partial(stay_kernel, shifts, share),
        out_shape=[
            jax.ShapeDtypeStruct(queries.shape, jnp.bfloat16),
            jax.ShapeDtypeStruct(queries.shape, jnp.bfloat16),
            jax.ShapeDtypeStruct(keys.shape, jnp.float32),
            jax.ShapeDtypeStruct(keys.shape, jnp.float32),
        ],
        grid=(steps,),
        in_specs=[wide, wide, narrow, narrow] + [narrow] * (2 * shifts) + [lead, stats],
        out_specs=[wide, wide, narrow, narrow],
        cost_estimate=pl.CostEstimate(
            flops=10 * queries.size * total,
            bytes_accessed=8 * queries.size,
            transcendentals=queries.size // HEAD_DIM * total,
        ),
        compiler_params=pltpu.CompilerParams(
            dimension_semantics=("arbitrary",), vmem_limit_bytes=VMEM_LIMIT
        ),
    )(
        queries, grads, keys, values, *earlier, prefix,
        pltpu.with_memory_space_constraint(marks, pltpu.HBM),
    )


def prepare_kernel(comp_span, length_ref, g_ref, *refs):
    sources, g_out, targets, sems = refs[:3], refs[3], refs[4:7], refs[7]
    copies = [pltpu.make_async_copy(a, b, sems.at[n]) for n, (a, b) in enumerate(zip(sources, targets))]

    @pl.when(pl.program_id(0) == 0)
    def _():
        for copy in copies:
            copy.start()

    rows, width = g_ref.shape
    length = length_ref[0, 0]
    ratio = jnp.float32(comp_span) / length.astype(jnp.float32)
    token = lax.axis_index("fsdp") * rows + lax.broadcasted_iota(jnp.int32, (rows, HEAD_DIM), 0)
    weight = jnp.where(token < length, ratio, jnp.float32(0.0))
    for at in range(0, width, HEAD_DIM):
        c = slice(at, at + HEAD_DIM)
        g_out[:, c] = (g_ref[:, c].astype(jnp.float32) * weight).astype(jnp.bfloat16)

    @pl.when(pl.program_id(0) == pl.num_programs(0) - 1)
    def _():
        for copy in copies:
            copy.wait()


def prepare(lengths, queries, grads, keys, values, comp_span):
    rows, width = grads.shape
    parts = PARTS if width % (PARTS * HEAD_DIM) == 0 else 1
    wide = pl.BlockSpec((rows, width // parts), lambda i: (0, i))
    whole = pl.BlockSpec(memory_space=pl.ANY)
    arrays = [pltpu.with_memory_space_constraint(x, pltpu.HBM) for x in (grads, queries, keys, values)]
    moved = 2 * 2 * (queries.size + grads.size + keys.size + values.size)
    g, q, k, v = pl.pallas_call(
        functools.partial(prepare_kernel, comp_span),
        out_shape=[jax.ShapeDtypeStruct(x.shape, x.dtype) for x in arrays],
        grid=(parts,),
        in_specs=[pl.BlockSpec(memory_space=pltpu.SMEM), wide, whole, whole, whole],
        out_specs=[wide, whole, whole, whole],
        scratch_shapes=[pltpu.SemaphoreType.DMA((3,))],
        cost_estimate=pl.CostEstimate(flops=grads.size, bytes_accessed=moved, transcendentals=0),
        compiler_params=pltpu.CompilerParams(
            dimension_semantics=("arbitrary",), vmem_limit_bytes=VMEM_LIMIT
        ),
    )(lengths, *arrays)
    return q, g, k, v


def shards(
    queries, completion_keys, completion_values, prompt_keys, prompt_values, output_grad, lengths
):
    fsdp = lax.axis_size("fsdp")
    everyone = fsdp * lax.axis_size("sample")
    rows = queries.shape[2]
    keys, values = completion_keys[0, 0], completion_values[0, 0]
    earlier = []
    for s in range(1, fsdp):
        ring = [(i, (i + s) % fsdp) for i in range(fsdp)]
        earlier += [lax.ppermute(keys, "fsdp", ring), lax.ppermute(values, "fsdp", ring)]
    line = jnp.stack([prompt_keys[0], prompt_values[0]], 1).astype(jnp.float32)
    prefix = lax.all_to_all(
        jnp.tile(line, (everyone, 1, 1)),
        ("sample", "fsdp"),
        split_axis=0,
        concat_axis=0,
        tiled=True,
    )
    q, g, k, v = prepare(lengths, queries[0, 0], output_grad[0, 0], keys, values, rows * fsdp)
    dback, dprefix, marks = travel(q, g, k, v, earlier, prefix)
    landed = []
    for s in range(1, fsdp):
        ring = [(i, (i - s) % fsdp) for i in range(fsdp)]
        landed.append(lax.ppermute(dback[s - 1], "fsdp", ring))
    shares = lax.all_to_all(dprefix, ("sample", "fsdp"), split_axis=0, concat_axis=0, tiled=True)
    out, dq, dk, dv = stay(q, g, k, v, earlier, prefix, marks)
    for block in landed:
        block = block.astype(jnp.float32)
        dk, dv = dk + block[0], dv + block[1]
    total = jnp.sum(shares.reshape((everyone, -1) + shares.shape[1:]), 0)
    return (
        out[None, None],
        dq[None, None],
        dk[None, None],
        dv[None, None],
        total[None, :, 0],
        total[None, :, 1],
    )


def solution(mesh):
    wide = P(("groups", "prompt"), "sample", "fsdp", None)
    lead = P(("groups", "prompt"), ("sample", "fsdp"), None)
    in_specs = (wide, wide, wide, lead, lead, wide, P(("groups", "prompt"), "sample"))
    out_specs = (wide, wide, wide, wide, lead, lead)
    return jax.shard_map(shards, mesh=mesh, in_specs=in_specs, out_specs=out_specs, check_vma=False)
```

```python
import functools

import jax
import jax.numpy as jnp
from jax import lax
from jax.experimental import pallas as pl
from jax.experimental.pallas import tpu as pltpu
from jax.sharding import PartitionSpec as P

HEAD_DIM = 128
LOG2E = 1.4426950408889634
UNITS = 2
PARTS = 4
VMEM_LIMIT = 24 << 20

NT = (((1,), (1,)), ((), ()))
NN = (((1,), (0,)), ((), ()))


def mm(a, b, dims=NN):
    return lax.dot_general(a, b, dims, preferred_element_type=jnp.float32)


def pad_rows(x, rows):
    if x.shape[0] == rows:
        return x
    return jnp.concatenate([x, jnp.zeros((rows - x.shape[0], x.shape[1]), x.dtype)], 0)


def geometry(q_ref, prefix, k_ref, shifts, share):
    rows = q_ref.shape[0]
    prompt = prefix.shape[0]
    padded = -(-prompt // 16) * 16
    chunk = min(rows, 256 // share)
    return rows, prompt, padded, padded + shifts * rows, chunk, k_ref.shape[1] // HEAD_DIM


def sides_of(units, padded, prefix, earlier, k_ref, v_ref):
    sides = []
    for u in range(units):
        col = slice(u * HEAD_DIM, (u + 1) * HEAD_DIM)
        pair = []
        for which, own in enumerate((k_ref, v_ref)):
            lead = pad_rows(prefix[:, which, col], padded).astype(jnp.bfloat16)
            past = [block[:, col] for block in earlier[which::2]]
            pair.append(jnp.concatenate([lead] + past + [own[:, col]], 0))
        sides.append(pair)
    return sides


def stacked(ref, u, share, part):
    return jnp.concatenate(
        [
            ref[part, (u * share + h) * HEAD_DIM : (u * share + h + 1) * HEAD_DIM]
            for h in range(share)
        ],
        0,
    )


def pieces(scores, seen, chunk, rows, prompt, padded, before, shifts):
    lead = scores[:prompt]
    back = [scores[padded + s * rows : padded + (s + 1) * rows] for s in range(shifts)]
    full = scores[before : seen - chunk]
    key = lax.broadcasted_iota(jnp.int32, (chunk, scores.shape[1]), 0)
    token = lax.rem(lax.broadcasted_iota(jnp.int32, (chunk, scores.shape[1]), 1), chunk)
    last = jnp.where(key <= token, scores[seen - chunk :], jnp.float32(-jnp.inf))
    return lead, back, full, last


def exponents(parts, top, bias, factor, padded):
    lead, back, full, last = parts
    out = [jnp.exp2(lead * factor - top)]
    if padded != lead.shape[0]:
        out.append(jnp.zeros((padded - lead.shape[0], lead.shape[1]), jnp.float32))
    out += [jnp.exp2(b * factor - (top - o)) for b, o in zip(back, bias)]
    if full.shape[0]:
        out.append(jnp.exp2(full * factor - top))
    out.append(jnp.exp2(last * factor - top))
    return jnp.concatenate(out, 0)


def biases(shifts):
    place = lax.axis_index("fsdp")
    return [
        jnp.where(place >= s + 1, jnp.float32(0.0), jnp.float32(-jnp.inf)) for s in range(shifts)
    ]


def grown(acc, new):
    if acc is None:
        return new
    old = acc[0].shape[0]
    return tuple(
        jnp.concatenate([a + n[:old], n[old:]], 0) if n.shape[0] > old else a + n
        for a, n in zip(acc, new)
    )


def pipeline(order, first, second, third):
    ahead, behind = first(*order[0]), None
    for n, (u, i) in enumerate(order):
        now = ahead
        if n + 1 < len(order):
            ahead = first(*order[n + 1])
        if behind is not None:
            third(*behind)
        behind = (u, i) + second(u, i, *now)
    third(*behind)


def travel_kernel(shifts, share, q_ref, g_ref, k_ref, v_ref, *refs):
    earlier, prefix = refs[: 2 * shifts], refs[2 * shifts]
    rest = refs[2 * shifts + 1 :]
    dback = rest[0] if shifts else None
    dprefix, stats = rest[-2:]
    rows, prompt, padded, before, chunk, units = geometry(q_ref, prefix, k_ref, shifts, share)
    steps = rows // chunk
    scale = HEAD_DIM ** -0.5
    factor = scale * LOG2E
    bias = biases(shifts)
    sides = sides_of(units, padded, prefix, earlier, k_ref, v_ref)
    acc = [None] * units

    def first(u, i):
        keys, values = sides[u]
        part = slice(i * chunk, (i + 1) * chunk)
        q, g = stacked(q_ref, u, share, part), stacked(g_ref, u, share, part)
        seen = before + (i + 1) * chunk
        return q, g, mm(keys[:seen], q, NT), mm(values[:seen], g, NT)

    def second(u, i, q, g, scores, dprob):
        seen = before + (i + 1) * chunk
        parts = pieces(scores, seen, chunk, rows, prompt, padded, before, shifts)
        lead, back, full, last = parts
        top = jnp.maximum(jnp.max(last, 0, keepdims=True), jnp.max(lead, 0, keepdims=True))
        if i:
            top = jnp.maximum(top, jnp.max(full, 0, keepdims=True))
        for s in range(shifts):
            top = jnp.maximum(top, jnp.max(back[s], 0, keepdims=True) + bias[s])
        top = top * factor
        expo = exponents(parts, top, bias, factor, padded)
        inverse = 1.0 / jnp.sum(expo, 0, keepdims=True)
        dot = jnp.sum(expo * dprob, 0, keepdims=True) * inverse
        n = u * steps + i
        stats[n, 0:1] = top
        stats[n, 1:2] = inverse
        stats[n, 2:3] = dot
        probs = expo[:before] * inverse
        sgrad = (probs * (dprob[:before] - dot)).astype(jnp.bfloat16)
        return q, g, probs.astype(jnp.bfloat16), sgrad

    def third(u, i, q, g, probs, sgrad):
        acc[u] = grown(acc[u], (mm(sgrad, q), mm(probs, g)))
        if i < steps - 1:
            return
        col = slice(u * HEAD_DIM, (u + 1) * HEAD_DIM)
        key_term, value_term = acc[u][0] * scale, acc[u][1]
        for s in range(shifts):
            at = slice(padded + s * rows, padded + (s + 1) * rows)
            dback[s, 0, :, col] = key_term[at].astype(jnp.bfloat16)
            dback[s, 1, :, col] = value_term[at].astype(jnp.bfloat16)
        dprefix[:, 0, col] = key_term[:prompt]
        dprefix[:, 1, col] = value_term[:prompt]

    pipeline([(u, i) for u in range(units) for i in range(steps)], first, second, third)


def stay_kernel(shifts, share, q_ref, g_ref, k_ref, v_ref, *refs):
    earlier, prefix, stats = refs[: 2 * shifts], refs[2 * shifts], refs[2 * shifts + 1]
    out, dq, dk, dv = refs[2 * shifts + 2 :]
    rows, prompt, padded, before, chunk, units = geometry(q_ref, prefix, k_ref, shifts, share)
    steps = rows // chunk
    scale = HEAD_DIM ** -0.5
    factor = scale * LOG2E
    bias = biases(shifts)
    sides = [
        (keys, values, keys.T, values.T)
        for keys, values in sides_of(units, padded, prefix, earlier, k_ref, v_ref)
    ]
    acc = [None] * units

    def first(u, i):
        keys, values = sides[u][:2]
        part = slice(i * chunk, (i + 1) * chunk)
        q, g = stacked(q_ref, u, share, part), stacked(g_ref, u, share, part)
        seen = before + (i + 1) * chunk
        return q, g, mm(keys[:seen], q, NT), mm(values[:seen], g, NT)

    def second(u, i, q, g, scores, dprob):
        seen = before + (i + 1) * chunk
        n = u * steps + i
        top, inverse, dot = stats[n, 0:1], stats[n, 1:2], stats[n, 2:3]
        parts = pieces(scores, seen, chunk, rows, prompt, padded, before, shifts)
        probs = exponents(parts, top, bias, factor, padded) * inverse
        sgrad = (probs * (dprob - dot)).astype(jnp.bfloat16)
        return q, g, probs.astype(jnp.bfloat16), sgrad

    def deep(left, right):
        total = None
        for at in range(0, right.shape[0], 256):
            end = min(at + 256, right.shape[0])
            term = mm(left[:, at:end], right[at:end])
            total = term if total is None else total + term
        return total

    def third(u, i, q, g, probs, sgrad):
        keys_t, values_t = sides[u][2:]
        seen = before + (i + 1) * chunk
        part = slice(i * chunk, (i + 1) * chunk)
        mixed = deep(values_t[:, :seen], probs).astype(jnp.bfloat16).T
        dquery = (deep(keys_t[:, :seen], sgrad) * scale).astype(jnp.bfloat16).T
        for h in range(share):
            c = slice((u * share + h) * HEAD_DIM, (u * share + h + 1) * HEAD_DIM)
            out[part, c] = mixed[h * chunk : (h + 1) * chunk]
            dq[part, c] = dquery[h * chunk : (h + 1) * chunk]
        acc[u] = grown(acc[u], (mm(sgrad[before:], q), mm(probs[before:], g)))
        if i == steps - 1:
            col = slice(u * HEAD_DIM, (u + 1) * HEAD_DIM)
            dk[:, col] = acc[u][0] * scale
            dv[:, col] = acc[u][1]

    pipeline([(u, i) for u in range(units) for i in range(steps)], first, second, third)


def specs_of(queries, keys, prefix):
    rows, width = queries.shape
    groups = keys.shape[1] // HEAD_DIM
    share = width // HEAD_DIM // groups
    units = UNITS if groups % UNITS == 0 else 1
    chunks = rows // min(rows, 256 // share)
    columns = share * rows // chunks
    wide = pl.BlockSpec((rows, units * share * HEAD_DIM), lambda i: (0, i))
    narrow = pl.BlockSpec((rows, units * HEAD_DIM), lambda i: (0, i))
    lead = pl.BlockSpec((prefix.shape[0], 2, units * HEAD_DIM), lambda i: (0, 0, i))
    stats = pl.BlockSpec((units * chunks, 8, columns), lambda i: (i, 0, 0))
    stats_shape = pltpu.HBM((groups * chunks, 8, columns), jnp.float32)
    return groups // units, units, share, wide, narrow, lead, stats, stats_shape


def travel(queries, grads, keys, values, earlier, prefix):
    steps, units, share, wide, narrow, lead, stats, stats_shape = specs_of(queries, keys, prefix)
    rows = queries.shape[0]
    shifts = len(earlier) // 2
    outs, out_specs = [], []
    if shifts:
        outs.append(jax.ShapeDtypeStruct((shifts, 2) + keys.shape, jnp.bfloat16))
        out_specs.append(pl.BlockSpec((shifts, 2, rows, units * HEAD_DIM), lambda i: (0, 0, 0, i)))
    outs += [jax.ShapeDtypeStruct(prefix.shape, jnp.float32), stats_shape]
    out_specs += [lead, stats]
    result = pl.pallas_call(
        functools.partial(travel_kernel, shifts, share),
        out_shape=outs,
        grid=(steps,),
        in_specs=[wide, wide, narrow, narrow] + [narrow] * (2 * shifts) + [lead],
        out_specs=out_specs,
        compiler_params=pltpu.CompilerParams(
            dimension_semantics=("arbitrary",), vmem_limit_bytes=VMEM_LIMIT
        ),
    )(queries, grads, keys, values, *earlier, prefix)
    return result if shifts else [None] + list(result)


def stay(queries, grads, keys, values, earlier, prefix, marks):
    steps, _, share, wide, narrow, lead, stats, _ = specs_of(queries, keys, prefix)
    shifts = len(earlier) // 2
    total = keys.shape[0] * (1 + shifts) + prefix.shape[0]
    return pl.pallas_call(
        functools.partial(stay_kernel, shifts, share),
        out_shape=[
            jax.ShapeDtypeStruct(queries.shape, jnp.bfloat16),
            jax.ShapeDtypeStruct(queries.shape, jnp.bfloat16),
            jax.ShapeDtypeStruct(keys.shape, jnp.float32),
            jax.ShapeDtypeStruct(keys.shape, jnp.float32),
        ],
        grid=(steps,),
        in_specs=[wide, wide, narrow, narrow] + [narrow] * (2 * shifts) + [lead, stats],
        out_specs=[wide, wide, narrow, narrow],
        cost_estimate=pl.CostEstimate(
            flops=10 * queries.size * total,
            bytes_accessed=8 * queries.size,
            transcendentals=queries.size // HEAD_DIM * total,
        ),
        compiler_params=pltpu.CompilerParams(
            dimension_semantics=("arbitrary",), vmem_limit_bytes=VMEM_LIMIT
        ),
    )(
        queries, grads, keys, values, *earlier, prefix,
        pltpu.with_memory_space_constraint(marks, pltpu.HBM),
    )


def prepare_kernel(comp_span, length_ref, g_ref, *refs):
    sources, g_out, targets, sems = refs[:3], refs[3], refs[4:7], refs[7]
    copies = [pltpu.make_async_copy(a, b, sems.at[n]) for n, (a, b) in enumerate(zip(sources, targets))]

    @pl.when(pl.program_id(0) == 0)
    def _():
        for copy in copies:
            copy.start()

    rows, width = g_ref.shape
    length = length_ref[0, 0]
    ratio = jnp.float32(comp_span) / length.astype(jnp.float32)
    token = lax.axis_index("fsdp") * rows + lax.broadcasted_iota(jnp.int32, (rows, HEAD_DIM), 0)
    weight = jnp.where(token < length, ratio, jnp.float32(0.0))
    for at in range(0, width, HEAD_DIM):
        c = slice(at, at + HEAD_DIM)
        g_out[:, c] = (g_ref[:, c].astype(jnp.float32) * weight).astype(jnp.bfloat16)

    @pl.when(pl.program_id(0) == pl.num_programs(0) - 1)
    def _():
        for copy in copies:
            copy.wait()


def prepare(lengths, queries, grads, keys, values, comp_span):
    rows, width = grads.shape
    parts = PARTS if width % (PARTS * HEAD_DIM) == 0 else 1
    wide = pl.BlockSpec((rows, width // parts), lambda i: (0, i))
    whole = pl.BlockSpec(memory_space=pl.ANY)
    arrays = [pltpu.with_memory_space_constraint(x, pltpu.HBM) for x in (grads, queries, keys, values)]
    moved = 2 * 2 * (queries.size + grads.size + keys.size + values.size)
    g, q, k, v = pl.pallas_call(
        functools.partial(prepare_kernel, comp_span),
        out_shape=[jax.ShapeDtypeStruct(x.shape, x.dtype) for x in arrays],
        grid=(parts,),
        in_specs=[pl.BlockSpec(memory_space=pltpu.SMEM), wide, whole, whole, whole],
        out_specs=[wide, whole, whole, whole],
        scratch_shapes=[pltpu.SemaphoreType.DMA((3,))],
        cost_estimate=pl.CostEstimate(flops=grads.size, bytes_accessed=moved, transcendentals=0),
        compiler_params=pltpu.CompilerParams(
            dimension_semantics=("arbitrary",), vmem_limit_bytes=VMEM_LIMIT
        ),
    )(lengths, *arrays)
    return q, g, k, v


def finish_kernel(count, dk, dv, shares, *refs):
    blocks, (dk_out, dv_out, lead_k, lead_v) = refs[:count], refs[count:]
    key_term, value_term = dk[...], dv[...]
    for block in blocks:
        key_term += block[0].astype(jnp.float32)
        value_term += block[1].astype(jnp.float32)
    dk_out[...] = key_term
    dv_out[...] = value_term
    here = lead_k.shape[0]
    total = shares[:here]
    for at in range(here, shares.shape[0], here):
        total += shares[at : at + here]
    lead_k[...] = total[:, 0]
    lead_v[...] = total[:, 1]


def finish(dk, dv, shares, landed, here):
    lead = jax.ShapeDtypeStruct((here, shares.shape[2]), jnp.float32)
    whole = jax.ShapeDtypeStruct(dk.shape, jnp.float32)
    return pl.pallas_call(
        functools.partial(finish_kernel, len(landed)),
        out_shape=[whole, whole, lead, lead],
        compiler_params=pltpu.CompilerParams(vmem_limit_bytes=VMEM_LIMIT),
    )(dk, dv, shares, *landed)


def shards(
    queries, completion_keys, completion_values, prompt_keys, prompt_values, output_grad, lengths
):
    fsdp = lax.axis_size("fsdp")
    everyone = fsdp * lax.axis_size("sample")
    rows = queries.shape[2]
    keys, values = completion_keys[0, 0], completion_values[0, 0]
    earlier = []
    for s in range(1, fsdp):
        ring = [(i, (i + s) % fsdp) for i in range(fsdp)]
        earlier.append(lax.ppermute(keys, "fsdp", ring))
        earlier.append(lax.ppermute(values, "fsdp", ring))
    line = jnp.stack([prompt_keys[0], prompt_values[0]], 1).astype(jnp.float32)
    line = jnp.tile(line, (everyone, 1, 1))
    prefix = lax.all_to_all(line, ("sample", "fsdp"), split_axis=0, concat_axis=0, tiled=True)
    q, g, k, v = prepare(lengths, queries[0, 0], output_grad[0, 0], keys, values, rows * fsdp)
    dback, dprefix, marks = travel(q, g, k, v, earlier, prefix)
    landed = []
    for s in range(1, fsdp):
        ring = [(i, (i - s) % fsdp) for i in range(fsdp)]
        landed.append(lax.ppermute(dback[s - 1], "fsdp", ring))
    shares = lax.all_to_all(dprefix, ("sample", "fsdp"), split_axis=0, concat_axis=0, tiled=True)
    out, dq, dk, dv = stay(q, g, k, v, earlier, prefix, marks)
    dk, dv, lead_k, lead_v = finish(dk, dv, shares, landed, prompt_keys.shape[1])
    return (
        out[None, None],
        dq[None, None],
        dk[None, None],
        dv[None, None],
        lead_k[None],
        lead_v[None],
    )


def solution(mesh):
    wide = P(("groups", "prompt"), "sample", "fsdp", None)
    lead = P(("groups", "prompt"), ("sample", "fsdp"), None)
    in_specs = (wide, wide, wide, lead, lead, wide, P(("groups", "prompt"), "sample"))
    out_specs = (wide, wide, wide, wide, lead, lead)
    return jax.shard_map(shards, mesh=mesh, in_specs=in_specs, out_specs=out_specs, check_vma=False)
```

```python
import functools

import jax
import jax.numpy as jnp
from jax import lax
from jax.experimental import pallas as pl
from jax.experimental.pallas import tpu as pltpu
from jax.sharding import PartitionSpec as P

HEAD_DIM = 128
LOG2E = 1.4426950408889634
UNITS = 2
PARTS = 4
VMEM_LIMIT = 24 << 20

NT = (((1,), (1,)), ((), ()))
NN = (((1,), (0,)), ((), ()))


def mm(a, b, dims=NN):
    return lax.dot_general(a, b, dims, preferred_element_type=jnp.float32)


def pad_rows(x, rows):
    if x.shape[0] == rows:
        return x
    return jnp.concatenate([x, jnp.zeros((rows - x.shape[0], x.shape[1]), x.dtype)], 0)


def geometry(q_ref, prefix, k_ref, shifts, share):
    rows = q_ref.shape[0]
    prompt = prefix.shape[0]
    padded = -(-prompt // 16) * 16
    chunk = min(rows, 256 // share)
    return rows, prompt, padded, padded + shifts * rows, chunk, k_ref.shape[1] // HEAD_DIM


def sides_of(units, padded, prefix, earlier, k_ref, v_ref):
    sides = []
    for u in range(units):
        col = slice(u * HEAD_DIM, (u + 1) * HEAD_DIM)
        pair = []
        for which, own in enumerate((k_ref, v_ref)):
            lead = pad_rows(prefix[:, which, col], padded).astype(jnp.bfloat16)
            past = [block[:, col] for block in earlier[which::2]]
            pair.append(jnp.concatenate([lead] + past + [own[:, col]], 0))
        sides.append(pair)
    return sides


def stacked(ref, u, share, part):
    return jnp.concatenate(
        [
            ref[part, (u * share + h) * HEAD_DIM : (u * share + h + 1) * HEAD_DIM]
            for h in range(share)
        ],
        0,
    )


def pieces(scores, seen, chunk, rows, prompt, padded, before, shifts):
    lead = scores[:prompt]
    back = [scores[padded + s * rows : padded + (s + 1) * rows] for s in range(shifts)]
    full = scores[before : seen - chunk]
    key = lax.broadcasted_iota(jnp.int32, (chunk, scores.shape[1]), 0)
    token = lax.rem(lax.broadcasted_iota(jnp.int32, (chunk, scores.shape[1]), 1), chunk)
    last = jnp.where(key <= token, scores[seen - chunk :], jnp.float32(-jnp.inf))
    return lead, back, full, last


def exponents(parts, top, bias, factor, padded):
    lead, back, full, last = parts
    out = [jnp.exp2(lead * factor - top)]
    if padded != lead.shape[0]:
        out.append(jnp.zeros((padded - lead.shape[0], lead.shape[1]), jnp.float32))
    out += [jnp.exp2(b * factor - (top - o)) for b, o in zip(back, bias)]
    if full.shape[0]:
        out.append(jnp.exp2(full * factor - top))
    out.append(jnp.exp2(last * factor - top))
    return jnp.concatenate(out, 0)


def biases(shifts):
    place = lax.axis_index("fsdp")
    return [
        jnp.where(place >= s + 1, jnp.float32(0.0), jnp.float32(-jnp.inf)) for s in range(shifts)
    ]


def grown(acc, new):
    if acc is None:
        return new
    old = acc[0].shape[0]
    return tuple(
        jnp.concatenate([a + n[:old], n[old:]], 0) if n.shape[0] > old else a + n
        for a, n in zip(acc, new)
    )


def pipeline(order, first, second, third):
    ahead, behind = first(*order[0]), None
    for n, (u, i) in enumerate(order):
        now = ahead
        if n + 1 < len(order):
            ahead = first(*order[n + 1])
        if behind is not None:
            third(*behind)
        behind = (u, i) + second(u, i, *now)
    third(*behind)


def travel_kernel(shifts, share, q_ref, g_ref, k_ref, v_ref, *refs):
    earlier, prefix = refs[: 2 * shifts], refs[2 * shifts]
    rest = refs[2 * shifts + 1 :]
    dback = rest[0] if shifts else None
    dprefix, stats = rest[-2:]
    rows, prompt, padded, before, chunk, units = geometry(q_ref, prefix, k_ref, shifts, share)
    steps = rows // chunk
    scale = HEAD_DIM ** -0.5
    factor = scale * LOG2E
    bias = biases(shifts)
    sides = sides_of(units, padded, prefix, earlier, k_ref, v_ref)
    acc = [None] * units

    def first(u, i):
        keys, values = sides[u]
        part = slice(i * chunk, (i + 1) * chunk)
        q, g = stacked(q_ref, u, share, part), stacked(g_ref, u, share, part)
        seen = before + (i + 1) * chunk
        return q, g, mm(keys[:seen], q, NT), mm(values[:seen], g, NT)

    def second(u, i, q, g, scores, dprob):
        seen = before + (i + 1) * chunk
        parts = pieces(scores, seen, chunk, rows, prompt, padded, before, shifts)
        lead, back, full, last = parts
        top = jnp.maximum(jnp.max(last, 0, keepdims=True), jnp.max(lead, 0, keepdims=True))
        if i:
            top = jnp.maximum(top, jnp.max(full, 0, keepdims=True))
        for s in range(shifts):
            top = jnp.maximum(top, jnp.max(back[s], 0, keepdims=True) + bias[s])
        top = top * factor
        expo = exponents(parts, top, bias, factor, padded)
        inverse = 1.0 / jnp.sum(expo, 0, keepdims=True)
        dot = jnp.sum(expo * dprob, 0, keepdims=True) * inverse
        n = u * steps + i
        stats[n, 0:1] = top
        stats[n, 1:2] = inverse
        stats[n, 2:3] = dot
        probs = expo[:before] * inverse
        sgrad = (probs * (dprob[:before] - dot)).astype(jnp.bfloat16)
        return q, g, probs.astype(jnp.bfloat16), sgrad

    def third(u, i, q, g, probs, sgrad):
        acc[u] = grown(acc[u], (mm(sgrad, q), mm(probs, g)))
        if i < steps - 1:
            return
        col = slice(u * HEAD_DIM, (u + 1) * HEAD_DIM)
        key_term, value_term = acc[u][0] * scale, acc[u][1]
        for s in range(shifts):
            at = slice(padded + s * rows, padded + (s + 1) * rows)
            dback[s, 0, :, col] = key_term[at].astype(jnp.bfloat16)
            dback[s, 1, :, col] = value_term[at].astype(jnp.bfloat16)
        dprefix[:, 0, col] = key_term[:prompt]
        dprefix[:, 1, col] = value_term[:prompt]

    pipeline([(u, i) for u in range(units) for i in range(steps)], first, second, third)


def stay_kernel(shifts, share, q_ref, g_ref, k_ref, v_ref, *refs):
    earlier, prefix, stats = refs[: 2 * shifts], refs[2 * shifts], refs[2 * shifts + 1]
    out, dq, dk, dv = refs[2 * shifts + 2 :]
    rows, prompt, padded, before, chunk, units = geometry(q_ref, prefix, k_ref, shifts, share)
    steps = rows // chunk
    scale = HEAD_DIM ** -0.5
    factor = scale * LOG2E
    bias = biases(shifts)
    sides = [
        (keys, values, keys.T, values.T)
        for keys, values in sides_of(units, padded, prefix, earlier, k_ref, v_ref)
    ]
    acc = [None] * units

    def first(u, i):
        keys, values = sides[u][:2]
        part = slice(i * chunk, (i + 1) * chunk)
        q, g = stacked(q_ref, u, share, part), stacked(g_ref, u, share, part)
        seen = before + (i + 1) * chunk
        return q, g, mm(keys[:seen], q, NT), mm(values[:seen], g, NT)

    def second(u, i, q, g, scores, dprob):
        seen = before + (i + 1) * chunk
        n = u * steps + i
        top, inverse, dot = stats[n, 0:1], stats[n, 1:2], stats[n, 2:3]
        parts = pieces(scores, seen, chunk, rows, prompt, padded, before, shifts)
        probs = exponents(parts, top, bias, factor, padded) * inverse
        sgrad = (probs * (dprob - dot)).astype(jnp.bfloat16)
        return q, g, probs.astype(jnp.bfloat16), sgrad

    def deep(left, right):
        total = None
        for at in range(0, right.shape[0], 256):
            end = min(at + 256, right.shape[0])
            term = mm(left[:, at:end], right[at:end])
            total = term if total is None else total + term
        return total

    def third(u, i, q, g, probs, sgrad):
        keys_t, values_t = sides[u][2:]
        seen = before + (i + 1) * chunk
        part = slice(i * chunk, (i + 1) * chunk)
        mixed = deep(values_t[:, :seen], probs).astype(jnp.bfloat16).T
        dquery = (deep(keys_t[:, :seen], sgrad) * scale).astype(jnp.bfloat16).T
        for h in range(share):
            c = slice((u * share + h) * HEAD_DIM, (u * share + h + 1) * HEAD_DIM)
            out[part, c] = mixed[h * chunk : (h + 1) * chunk]
            dq[part, c] = dquery[h * chunk : (h + 1) * chunk]
        acc[u] = grown(acc[u], (mm(sgrad[before:], q), mm(probs[before:], g)))
        if i == steps - 1:
            col = slice(u * HEAD_DIM, (u + 1) * HEAD_DIM)
            dk[:, col] = acc[u][0] * scale
            dv[:, col] = acc[u][1]

    pipeline([(u, i) for u in range(units) for i in range(steps)], first, second, third)


def specs_of(queries, keys, prefix):
    rows, width = queries.shape
    groups = keys.shape[1] // HEAD_DIM
    share = width // HEAD_DIM // groups
    units = UNITS if groups % UNITS == 0 else 1
    chunks = rows // min(rows, 256 // share)
    columns = share * rows // chunks
    wide = pl.BlockSpec((rows, units * share * HEAD_DIM), lambda i: (0, i))
    narrow = pl.BlockSpec((rows, units * HEAD_DIM), lambda i: (0, i))
    lead = pl.BlockSpec((prefix.shape[0], 2, units * HEAD_DIM), lambda i: (0, 0, i))
    stats = pl.BlockSpec((units * chunks, 8, columns), lambda i: (i, 0, 0))
    stats_shape = pltpu.HBM((groups * chunks, 8, columns), jnp.float32)
    return groups // units, units, share, wide, narrow, lead, stats, stats_shape


def travel(queries, grads, keys, values, earlier, prefix):
    groups = keys.shape[1] // HEAD_DIM
    share = queries.shape[1] // HEAD_DIM // groups
    shifts = len(earlier) // 2
    outs = [jax.ShapeDtypeStruct((shifts, 2) + keys.shape, jnp.bfloat16)] if shifts else []
    outs.append(jax.ShapeDtypeStruct(prefix.shape, jnp.float32))
    outs.append(specs_of(queries, keys, prefix)[-1])
    arrays = [
        pltpu.with_memory_space_constraint(x, pltpu.VMEM)
        for x in (queries, grads, keys, values, *earlier, prefix)
    ]
    result = pl.pallas_call(
        functools.partial(travel_kernel, shifts, share),
        out_shape=outs,
        in_specs=[pl.BlockSpec(memory_space=pltpu.VMEM)] * len(arrays),
        out_specs=[pl.BlockSpec(memory_space=pltpu.VMEM)] * len(outs),
        compiler_params=pltpu.CompilerParams(vmem_limit_bytes=VMEM_LIMIT),
    )(*arrays)
    return result if shifts else [None] + list(result)


def stay(queries, grads, keys, values, earlier, prefix, marks):
    steps, _, share, wide, narrow, lead, stats, _ = specs_of(queries, keys, prefix)
    shifts = len(earlier) // 2
    total = keys.shape[0] * (1 + shifts) + prefix.shape[0]
    return pl.pallas_call(
        functools.partial(stay_kernel, shifts, share),
        out_shape=[
            jax.ShapeDtypeStruct(queries.shape, jnp.bfloat16),
            jax.ShapeDtypeStruct(queries.shape, jnp.bfloat16),
            jax.ShapeDtypeStruct(keys.shape, jnp.float32),
            jax.ShapeDtypeStruct(keys.shape, jnp.float32),
        ],
        grid=(steps,),
        in_specs=[wide, wide, narrow, narrow] + [narrow] * (2 * shifts) + [lead, stats],
        out_specs=[wide, wide, narrow, narrow],
        cost_estimate=pl.CostEstimate(
            flops=10 * queries.size * total,
            bytes_accessed=8 * queries.size,
            transcendentals=queries.size // HEAD_DIM * total,
        ),
        compiler_params=pltpu.CompilerParams(
            dimension_semantics=("arbitrary",), vmem_limit_bytes=VMEM_LIMIT
        ),
    )(
        queries, grads, keys, values, *earlier, prefix,
        pltpu.with_memory_space_constraint(marks, pltpu.HBM),
    )


def prepare_kernel(comp_span, length_ref, g_ref, *refs):
    sources, g_out, targets, sems = refs[:3], refs[3], refs[4:7], refs[7]
    copies = [pltpu.make_async_copy(a, b, sems.at[n]) for n, (a, b) in enumerate(zip(sources, targets))]

    @pl.when(pl.program_id(0) == 0)
    def _():
        for copy in copies:
            copy.start()

    rows, width = g_ref.shape
    length = length_ref[0, 0]
    ratio = jnp.float32(comp_span) / length.astype(jnp.float32)
    token = lax.axis_index("fsdp") * rows + lax.broadcasted_iota(jnp.int32, (rows, HEAD_DIM), 0)
    weight = jnp.where(token < length, ratio, jnp.float32(0.0))
    for at in range(0, width, HEAD_DIM):
        c = slice(at, at + HEAD_DIM)
        g_out[:, c] = (g_ref[:, c].astype(jnp.float32) * weight).astype(jnp.bfloat16)

    @pl.when(pl.program_id(0) == pl.num_programs(0) - 1)
    def _():
        for copy in copies:
            copy.wait()


def prepare(lengths, queries, grads, keys, values, comp_span):
    rows, width = grads.shape
    parts = PARTS if width % (PARTS * HEAD_DIM) == 0 else 1
    wide = pl.BlockSpec((rows, width // parts), lambda i: (0, i))
    whole = pl.BlockSpec(memory_space=pl.ANY)
    arrays = [pltpu.with_memory_space_constraint(x, pltpu.HBM) for x in (grads, queries, keys, values)]
    moved = 2 * 2 * (queries.size + grads.size + keys.size + values.size)
    g, q, k, v = pl.pallas_call(
        functools.partial(prepare_kernel, comp_span),
        out_shape=[jax.ShapeDtypeStruct(x.shape, x.dtype) for x in arrays],
        grid=(parts,),
        in_specs=[pl.BlockSpec(memory_space=pltpu.SMEM), wide, whole, whole, whole],
        out_specs=[wide, whole, whole, whole],
        scratch_shapes=[pltpu.SemaphoreType.DMA((3,))],
        cost_estimate=pl.CostEstimate(flops=grads.size, bytes_accessed=moved, transcendentals=0),
        compiler_params=pltpu.CompilerParams(
            dimension_semantics=("arbitrary",), vmem_limit_bytes=VMEM_LIMIT
        ),
    )(lengths, *arrays)
    return q, g, k, v


def finish_kernel(count, dk, dv, shares, *refs):
    blocks, (dk_out, dv_out, lead_k, lead_v) = refs[:count], refs[count:]
    key_term, value_term = dk[...], dv[...]
    for block in blocks:
        key_term += block[0].astype(jnp.float32)
        value_term += block[1].astype(jnp.float32)
    dk_out[...] = key_term
    dv_out[...] = value_term
    here = lead_k.shape[0]
    total = shares[:here]
    for at in range(here, shares.shape[0], here):
        total += shares[at : at + here]
    lead_k[...] = total[:, 0]
    lead_v[...] = total[:, 1]


def finish(dk, dv, shares, landed, here):
    lead = jax.ShapeDtypeStruct((here, shares.shape[2]), jnp.float32)
    whole = jax.ShapeDtypeStruct(dk.shape, jnp.float32)
    return pl.pallas_call(
        functools.partial(finish_kernel, len(landed)),
        out_shape=[whole, whole, lead, lead],
        compiler_params=pltpu.CompilerParams(vmem_limit_bytes=VMEM_LIMIT),
    )(dk, dv, shares, *landed)


def shards(
    queries, completion_keys, completion_values, prompt_keys, prompt_values, output_grad, lengths
):
    fsdp = lax.axis_size("fsdp")
    everyone = fsdp * lax.axis_size("sample")
    rows = queries.shape[2]
    keys, values = completion_keys[0, 0], completion_values[0, 0]
    earlier = []
    for s in range(1, fsdp):
        ring = [(i, (i + s) % fsdp) for i in range(fsdp)]
        earlier.append(lax.ppermute(keys, "fsdp", ring))
        earlier.append(lax.ppermute(values, "fsdp", ring))
    line = jnp.stack([prompt_keys[0], prompt_values[0]], 1).astype(jnp.float32)
    line = jnp.tile(line, (everyone, 1, 1))
    prefix = lax.all_to_all(line, ("sample", "fsdp"), split_axis=0, concat_axis=0, tiled=True)
    q, g, k, v = prepare(lengths, queries[0, 0], output_grad[0, 0], keys, values, rows * fsdp)
    dback, dprefix, marks = travel(q, g, k, v, earlier, prefix)
    landed = []
    for s in range(1, fsdp):
        ring = [(i, (i - s) % fsdp) for i in range(fsdp)]
        landed.append(lax.ppermute(dback[s - 1], "fsdp", ring))
    shares = lax.all_to_all(dprefix, ("sample", "fsdp"), split_axis=0, concat_axis=0, tiled=True)
    out, dq, dk, dv = stay(q, g, k, v, earlier, prefix, marks)
    dk, dv, lead_k, lead_v = finish(dk, dv, shares, landed, prompt_keys.shape[1])
    return (
        out[None, None],
        dq[None, None],
        dk[None, None],
        dv[None, None],
        lead_k[None],
        lead_v[None],
    )


def solution(mesh):
    wide = P(("groups", "prompt"), "sample", "fsdp", None)
    lead = P(("groups", "prompt"), ("sample", "fsdp"), None)
    in_specs = (wide, wide, wide, lead, lead, wide, P(("groups", "prompt"), "sample"))
    out_specs = (wide, wide, wide, wide, lead, lead)
    return jax.shard_map(shards, mesh=mesh, in_specs=in_specs, out_specs=out_specs, check_vma=False)
```

```python
import functools

import jax
import jax.numpy as jnp
from jax import lax
from jax.experimental import pallas as pl
from jax.experimental.pallas import tpu as pltpu
from jax.sharding import PartitionSpec as P

HEAD_DIM = 128
LOG2E = 1.4426950408889634
UNITS = 2
PARTS = 2
VMEM_LIMIT = 24 << 20

NT = (((1,), (1,)), ((), ()))
NN = (((1,), (0,)), ((), ()))


def mm(a, b, dims=NN):
    return lax.dot_general(a, b, dims, preferred_element_type=jnp.float32)


def pad_rows(x, rows):
    if x.shape[0] == rows:
        return x
    return jnp.concatenate([x, jnp.zeros((rows - x.shape[0], x.shape[1]), x.dtype)], 0)


def geometry(q_ref, prefix, k_ref, shifts, share):
    rows = q_ref.shape[0]
    prompt = prefix.shape[0]
    padded = -(-prompt // 16) * 16
    chunk = min(rows, 256 // share)
    return rows, prompt, padded, padded + shifts * rows, chunk, k_ref.shape[1] // HEAD_DIM


def sides_of(units, padded, prefix, earlier, k_ref, v_ref):
    sides = []
    for u in range(units):
        col = slice(u * HEAD_DIM, (u + 1) * HEAD_DIM)
        pair = []
        for which, own in enumerate((k_ref, v_ref)):
            lead = pad_rows(prefix[:, which, col], padded).astype(jnp.bfloat16)
            past = [block[:, col] for block in earlier[which::2]]
            pair.append(jnp.concatenate([lead] + past + [own[:, col]], 0))
        sides.append(pair)
    return sides


def stacked(ref, u, share, part):
    return jnp.concatenate(
        [
            ref[part, (u * share + h) * HEAD_DIM : (u * share + h + 1) * HEAD_DIM]
            for h in range(share)
        ],
        0,
    )


def pieces(scores, seen, chunk, rows, prompt, padded, before, shifts):
    lead = scores[:prompt]
    back = [scores[padded + s * rows : padded + (s + 1) * rows] for s in range(shifts)]
    full = scores[before : seen - chunk]
    key = lax.broadcasted_iota(jnp.int32, (chunk, scores.shape[1]), 0)
    token = lax.rem(lax.broadcasted_iota(jnp.int32, (chunk, scores.shape[1]), 1), chunk)
    last = jnp.where(key <= token, scores[seen - chunk :], jnp.float32(-jnp.inf))
    return lead, back, full, last


def exponents(parts, top, bias, factor, padded):
    lead, back, full, last = parts
    out = [jnp.exp2(lead * factor - top)]
    if padded != lead.shape[0]:
        out.append(jnp.zeros((padded - lead.shape[0], lead.shape[1]), jnp.float32))
    out += [jnp.exp2(b * factor - (top - o)) for b, o in zip(back, bias)]
    if full.shape[0]:
        out.append(jnp.exp2(full * factor - top))
    out.append(jnp.exp2(last * factor - top))
    return jnp.concatenate(out, 0)


def biases(shifts):
    place = lax.axis_index("fsdp")
    return [
        jnp.where(place >= s + 1, jnp.float32(0.0), jnp.float32(-jnp.inf)) for s in range(shifts)
    ]


def grown(acc, new):
    if acc is None:
        return new
    old = acc[0].shape[0]
    return tuple(
        jnp.concatenate([a + n[:old], n[old:]], 0) if n.shape[0] > old else a + n
        for a, n in zip(acc, new)
    )


def pipeline(order, first, second, third):
    ahead, behind = first(*order[0]), None
    for n, (u, i) in enumerate(order):
        now = ahead
        if n + 1 < len(order):
            ahead = first(*order[n + 1])
        if behind is not None:
            third(*behind)
        behind = (u, i) + second(u, i, *now)
    third(*behind)


def travel_kernel(shifts, share, q_ref, g_ref, k_ref, v_ref, *refs):
    earlier, prefix = refs[: 2 * shifts], refs[2 * shifts]
    rest = refs[2 * shifts + 1 :]
    dback = rest[0] if shifts else None
    dprefix, stats = rest[-2:]
    rows, prompt, padded, before, chunk, units = geometry(q_ref, prefix, k_ref, shifts, share)
    steps = rows // chunk
    scale = HEAD_DIM ** -0.5
    factor = scale * LOG2E
    bias = biases(shifts)
    sides = sides_of(units, padded, prefix, earlier, k_ref, v_ref)
    acc = [None] * units

    def first(u, i):
        keys, values = sides[u]
        part = slice(i * chunk, (i + 1) * chunk)
        q, g = stacked(q_ref, u, share, part), stacked(g_ref, u, share, part)
        seen = before + (i + 1) * chunk
        return q, g, mm(keys[:seen], q, NT), mm(values[:seen], g, NT)

    def second(u, i, q, g, scores, dprob):
        seen = before + (i + 1) * chunk
        parts = pieces(scores, seen, chunk, rows, prompt, padded, before, shifts)
        lead, back, full, last = parts
        top = jnp.maximum(jnp.max(last, 0, keepdims=True), jnp.max(lead, 0, keepdims=True))
        if i:
            top = jnp.maximum(top, jnp.max(full, 0, keepdims=True))
        for s in range(shifts):
            top = jnp.maximum(top, jnp.max(back[s], 0, keepdims=True) + bias[s])
        top = top * factor
        expo = exponents(parts, top, bias, factor, padded)
        inverse = 1.0 / jnp.sum(expo, 0, keepdims=True)
        dot = jnp.sum(expo * dprob, 0, keepdims=True) * inverse
        n = u * steps + i
        stats[n, 0:1] = top
        stats[n, 1:2] = inverse
        stats[n, 2:3] = dot
        probs = expo[:before] * inverse
        sgrad = (probs * (dprob[:before] - dot)).astype(jnp.bfloat16)
        return q, g, probs.astype(jnp.bfloat16), sgrad

    def third(u, i, q, g, probs, sgrad):
        acc[u] = grown(acc[u], (mm(sgrad, q), mm(probs, g)))
        if i < steps - 1:
            return
        col = slice(u * HEAD_DIM, (u + 1) * HEAD_DIM)
        key_term, value_term = acc[u][0] * scale, acc[u][1]
        for s in range(shifts):
            at = slice(padded + s * rows, padded + (s + 1) * rows)
            dback[s, 0, :, col] = key_term[at].astype(jnp.bfloat16)
            dback[s, 1, :, col] = value_term[at].astype(jnp.bfloat16)
        dprefix[:, 0, col] = key_term[:prompt]
        dprefix[:, 1, col] = value_term[:prompt]

    pipeline([(u, i) for u in range(units) for i in range(steps)], first, second, third)


def stay_kernel(shifts, share, q_ref, g_ref, k_ref, v_ref, *refs):
    earlier, prefix, stats = refs[: 2 * shifts], refs[2 * shifts], refs[2 * shifts + 1]
    out, dq, dk, dv = refs[2 * shifts + 2 :]
    span = dk.shape[1]
    at = pl.multiple_of(pl.program_id(0) * span, span)
    q_ref = q_ref.at[:, pl.ds(pl.multiple_of(at * share, span * share), span * share)]
    g_ref = g_ref.at[:, pl.ds(pl.multiple_of(at * share, span * share), span * share)]
    k_ref, v_ref = k_ref.at[:, pl.ds(at, span)], v_ref.at[:, pl.ds(at, span)]
    earlier = [block.at[:, pl.ds(at, span)] for block in earlier]
    prefix = prefix.at[:, :, pl.ds(at, span)]
    rows, prompt, padded, before, chunk, units = geometry(q_ref, prefix, k_ref, shifts, share)
    steps = rows // chunk
    scale = HEAD_DIM ** -0.5
    factor = scale * LOG2E
    bias = biases(shifts)
    sides = [
        (keys, values, keys.T, values.T)
        for keys, values in sides_of(units, padded, prefix, earlier, k_ref, v_ref)
    ]
    acc = [None] * units

    def first(u, i):
        keys, values = sides[u][:2]
        part = slice(i * chunk, (i + 1) * chunk)
        q, g = stacked(q_ref, u, share, part), stacked(g_ref, u, share, part)
        seen = before + (i + 1) * chunk
        return q, g, mm(keys[:seen], q, NT), mm(values[:seen], g, NT)

    def second(u, i, q, g, scores, dprob):
        seen = before + (i + 1) * chunk
        n = u * steps + i
        top, inverse, dot = stats[n, 0:1], stats[n, 1:2], stats[n, 2:3]
        parts = pieces(scores, seen, chunk, rows, prompt, padded, before, shifts)
        probs = exponents(parts, top, bias, factor, padded) * inverse
        sgrad = (probs * (dprob - dot)).astype(jnp.bfloat16)
        return q, g, probs.astype(jnp.bfloat16), sgrad

    def deep(left, right):
        total = None
        for at in range(0, right.shape[0], 256):
            end = min(at + 256, right.shape[0])
            term = mm(left[:, at:end], right[at:end])
            total = term if total is None else total + term
        return total

    def third(u, i, q, g, probs, sgrad):
        keys_t, values_t = sides[u][2:]
        seen = before + (i + 1) * chunk
        part = slice(i * chunk, (i + 1) * chunk)
        mixed = deep(values_t[:, :seen], probs).astype(jnp.bfloat16).T
        dquery = (deep(keys_t[:, :seen], sgrad) * scale).astype(jnp.bfloat16).T
        for h in range(share):
            c = slice((u * share + h) * HEAD_DIM, (u * share + h + 1) * HEAD_DIM)
            out[part, c] = mixed[h * chunk : (h + 1) * chunk]
            dq[part, c] = dquery[h * chunk : (h + 1) * chunk]
        acc[u] = grown(acc[u], (mm(sgrad[before:], q), mm(probs[before:], g)))
        if i == steps - 1:
            col = slice(u * HEAD_DIM, (u + 1) * HEAD_DIM)
            dk[:, col] = acc[u][0] * scale
            dv[:, col] = acc[u][1]

    pipeline([(u, i) for u in range(units) for i in range(steps)], first, second, third)


def specs_of(queries, keys, prefix):
    rows, width = queries.shape
    groups = keys.shape[1] // HEAD_DIM
    share = width // HEAD_DIM // groups
    units = UNITS if groups % UNITS == 0 else 1
    chunks = rows // min(rows, 256 // share)
    columns = share * rows // chunks
    wide = pl.BlockSpec((rows, units * share * HEAD_DIM), lambda i: (0, i))
    narrow = pl.BlockSpec((rows, units * HEAD_DIM), lambda i: (0, i))
    lead = pl.BlockSpec((prefix.shape[0], 2, units * HEAD_DIM), lambda i: (0, 0, i))
    stats = pl.BlockSpec((units * chunks, 8, columns), lambda i: (i, 0, 0))
    stats_shape = pltpu.HBM((groups * chunks, 8, columns), jnp.float32)
    return groups // units, units, share, wide, narrow, lead, stats, stats_shape


def travel(queries, grads, keys, values, earlier, prefix):
    groups = keys.shape[1] // HEAD_DIM
    share = queries.shape[1] // HEAD_DIM // groups
    shifts = len(earlier) // 2
    outs = [jax.ShapeDtypeStruct((shifts, 2) + keys.shape, jnp.bfloat16)] if shifts else []
    outs.append(jax.ShapeDtypeStruct(prefix.shape, jnp.float32))
    outs.append(specs_of(queries, keys, prefix)[-1])
    arrays = [
        pltpu.with_memory_space_constraint(x, pltpu.VMEM)
        for x in (queries, grads, keys, values, *earlier, prefix)
    ]
    result = pl.pallas_call(
        functools.partial(travel_kernel, shifts, share),
        out_shape=outs,
        in_specs=[pl.BlockSpec(memory_space=pltpu.VMEM)] * len(arrays),
        out_specs=[pl.BlockSpec(memory_space=pltpu.VMEM)] * len(outs),
        compiler_params=pltpu.CompilerParams(vmem_limit_bytes=VMEM_LIMIT),
    )(*arrays)
    return result if shifts else [None] + list(result)


def stay(queries, grads, keys, values, earlier, prefix, marks):
    steps, _, share, wide, narrow, _, stats, _ = specs_of(queries, keys, prefix)
    shifts = len(earlier) // 2
    total = keys.shape[0] * (1 + shifts) + prefix.shape[0]
    return pl.pallas_call(
        functools.partial(stay_kernel, shifts, share),
        out_shape=[
            jax.ShapeDtypeStruct(queries.shape, jnp.bfloat16),
            jax.ShapeDtypeStruct(queries.shape, jnp.bfloat16),
            jax.ShapeDtypeStruct(keys.shape, jnp.float32),
            jax.ShapeDtypeStruct(keys.shape, jnp.float32),
        ],
        grid=(steps,),
        in_specs=[pl.BlockSpec(memory_space=pltpu.VMEM)] * (5 + 2 * shifts) + [stats],
        out_specs=[wide, wide, narrow, narrow],
        cost_estimate=pl.CostEstimate(
            flops=10 * queries.size * total,
            bytes_accessed=8 * queries.size,
            transcendentals=queries.size // HEAD_DIM * total,
        ),
        compiler_params=pltpu.CompilerParams(
            dimension_semantics=("arbitrary",),
            vmem_limit_bytes=VMEM_LIMIT,
        ),
    )(
        *(
            pltpu.with_memory_space_constraint(x, pltpu.VMEM)
            for x in (queries, grads, keys, values, *earlier, prefix)
        ),
        pltpu.with_memory_space_constraint(marks, pltpu.HBM),
    )


def prepare_kernel(comp_span, length_ref, g_ref, *refs):
    sources, g_out, targets, sems = refs[:3], refs[3], refs[4:7], refs[7]
    copies = [pltpu.make_async_copy(a, b, sems.at[n]) for n, (a, b) in enumerate(zip(sources, targets))]

    @pl.when(pl.program_id(0) == 0)
    def _():
        for copy in copies:
            copy.start()

    rows, width = g_ref.shape
    length = length_ref[0, 0]
    ratio = jnp.float32(comp_span) / length.astype(jnp.float32)
    token = lax.axis_index("fsdp") * rows + lax.broadcasted_iota(jnp.int32, (rows, HEAD_DIM), 0)
    weight = jnp.where(token < length, ratio, jnp.float32(0.0))
    for at in range(0, width, HEAD_DIM):
        c = slice(at, at + HEAD_DIM)
        g_out[:, c] = (g_ref[:, c].astype(jnp.float32) * weight).astype(jnp.bfloat16)

    @pl.when(pl.program_id(0) == pl.num_programs(0) - 1)
    def _():
        for copy in copies:
            copy.wait()


def prepare(lengths, queries, grads, keys, values, comp_span):
    rows, width = grads.shape
    parts = PARTS if width % (PARTS * HEAD_DIM) == 0 else 1
    wide = pl.BlockSpec((rows, width // parts), lambda i: (0, i))
    whole = pl.BlockSpec(memory_space=pl.ANY)
    arrays = [pltpu.with_memory_space_constraint(x, pltpu.HBM) for x in (grads, queries, keys, values)]
    moved = 2 * 2 * (queries.size + grads.size + keys.size + values.size)
    g, q, k, v = pl.pallas_call(
        functools.partial(prepare_kernel, comp_span),
        out_shape=[jax.ShapeDtypeStruct(x.shape, x.dtype) for x in arrays],
        grid=(parts,),
        in_specs=[pl.BlockSpec(memory_space=pltpu.SMEM), wide, whole, whole, whole],
        out_specs=[wide, whole, whole, whole],
        scratch_shapes=[pltpu.SemaphoreType.DMA((3,))],
        cost_estimate=pl.CostEstimate(flops=grads.size, bytes_accessed=moved, transcendentals=0),
        compiler_params=pltpu.CompilerParams(
            dimension_semantics=("arbitrary",), vmem_limit_bytes=VMEM_LIMIT
        ),
    )(lengths, *arrays)
    return q, g, k, v


def finish_kernel(count, dk, dv, shares, *refs):
    blocks, (dk_out, dv_out, lead_k, lead_v) = refs[:count], refs[count:]
    key_term, value_term = dk[...], dv[...]
    for block in blocks:
        key_term += block[0].astype(jnp.float32)
        value_term += block[1].astype(jnp.float32)
    dk_out[...] = key_term
    dv_out[...] = value_term
    here = lead_k.shape[0]
    total = shares[:here]
    for at in range(here, shares.shape[0], here):
        total += shares[at : at + here]
    lead_k[...] = total[:, 0]
    lead_v[...] = total[:, 1]


def finish(dk, dv, shares, landed, here):
    lead = jax.ShapeDtypeStruct((here, shares.shape[2]), jnp.float32)
    whole = jax.ShapeDtypeStruct(dk.shape, jnp.float32)
    return pl.pallas_call(
        functools.partial(finish_kernel, len(landed)),
        out_shape=[whole, whole, lead, lead],
        compiler_params=pltpu.CompilerParams(vmem_limit_bytes=VMEM_LIMIT),
    )(dk, dv, shares, *landed)


def shards(
    queries, completion_keys, completion_values, prompt_keys, prompt_values, output_grad, lengths
):
    fsdp = lax.axis_size("fsdp")
    everyone = fsdp * lax.axis_size("sample")
    rows = queries.shape[2]
    keys, values = completion_keys[0, 0], completion_values[0, 0]
    earlier = []
    for s in range(1, fsdp):
        ring = [(i, (i + s) % fsdp) for i in range(fsdp)]
        earlier.append(lax.ppermute(keys, "fsdp", ring))
        earlier.append(lax.ppermute(values, "fsdp", ring))
    line = jnp.stack([prompt_keys[0], prompt_values[0]], 1).astype(jnp.float32)
    line = jnp.tile(line, (everyone, 1, 1))
    prefix = lax.all_to_all(line, ("sample", "fsdp"), split_axis=0, concat_axis=0, tiled=True)
    q, g, k, v = prepare(lengths, queries[0, 0], output_grad[0, 0], keys, values, rows * fsdp)
    dback, dprefix, marks = travel(q, g, k, v, earlier, prefix)
    landed = []
    for s in range(1, fsdp):
        ring = [(i, (i - s) % fsdp) for i in range(fsdp)]
        landed.append(lax.ppermute(dback[s - 1], "fsdp", ring))
    shares = lax.all_to_all(dprefix, ("sample", "fsdp"), split_axis=0, concat_axis=0, tiled=True)
    out, dq, dk, dv = stay(q, g, k, v, earlier, prefix, marks)
    dk, dv, lead_k, lead_v = finish(dk, dv, shares, landed, prompt_keys.shape[1])
    return (
        out[None, None],
        dq[None, None],
        dk[None, None],
        dv[None, None],
        lead_k[None],
        lead_v[None],
    )


def solution(mesh):
    wide = P(("groups", "prompt"), "sample", "fsdp", None)
    lead = P(("groups", "prompt"), ("sample", "fsdp"), None)
    in_specs = (wide, wide, wide, lead, lead, wide, P(("groups", "prompt"), "sample"))
    out_specs = (wide, wide, wide, wide, lead, lead)
    return jax.shard_map(shards, mesh=mesh, in_specs=in_specs, out_specs=out_specs, check_vma=False)
```
